32 devices in a mesh: row: 4 (over x, core), col: 8 (over z, y).
Axes of the slice: x: 2, y: 2, z: 4, core: 2. Of those that a mesh axis runs over, the one named last changes fastest.
Arguments:
- front_panels: float32 [16, 4, 256, 8, 8, 256], P(None, 'row', 'col'), as said below
- child_update_tiles: float32 [4, 8, 8, 256, 256], P('row', 'col'), may hold values from -2 to 2
- child_rows: int32 [4, 8, 8], P('row', 'col'), may hold values from 0 to 63, as said below
- child_cols: int32 [4, 8, 8], P('row', 'col'), may hold values from 0 to 7
- child_counts: int32 [4, 8], P('row', 'col'), may hold values from 4 to 8, as said below
- row_maps: int32 [4, 8, 8, 256], P('row', 'col'), may hold values from 0 to 255, each once within a row
- col_maps: int32 [4, 8, 8, 256], P('row', 'col'), may hold values from 0 to 255, each once within a row
Outputs:
- factored_front: float32 [16, 4, 256, 8, 8, 256], P(None, 'row', None, None, 'col')
The draws below stay inside these ranges and needn't reach their ends.
Inputs may be any that keep to these rules, and one draw needn't show every extreme that they name: child_rows[r, c, k] modulo 4 names one of four owner rows; among the live slots of one device at most 2 name the same owner row, and some device sends exactly 2 to some owner; every slot's target tile column is at most its target tile row. `child_counts`: every device of col index 0 has all slots live. `front_panels`: the diagonal of the front dominates its first tile, so that tile stays positive definite after the children are added.
All inputs are finite; a program needn't handle non-finite values.
Results may differ from the reference program's by a relative error of at most 0.0003.
Values sent between devices are 32-bit elements; how exact they have to be, the bound alone decides.
No kernel may reach another device: no remote copies, remote signals or barrier semaphores. Data moves between devices by JAX's collectives and lax.ppermute only.
A program may use at most 320 MiB of HBM per device.

```python
import jax
import jax.numpy as jnp
from jax import lax

TILE = 256
FRONT = 16384
CHILD = 8
ROW_TILES = 16
COL_TILES = 8
N_ROW = 4
N_COL = 8


def child_layout(key):
    base_key = jax.random.fold_in(key, 101)
    start = jax.random.randint(jax.random.fold_in(base_key, 1), (1, N_COL, 1), 0, N_ROW)
    slot_ids = lax.broadcasted_iota(jnp.int32, (N_ROW, N_COL, CHILD), 2)
    col_ids = lax.broadcasted_iota(jnp.int32, (N_ROW, N_COL, CHILD), 1)
    owners = (start + slot_ids // (CHILD // 4)) % N_ROW
    tile_cols = jax.random.randint(jax.random.fold_in(base_key, 3), (N_ROW, N_COL, CHILD), 0, COL_TILES)
    highest_row = owners + N_ROW * (ROW_TILES - 1)
    tile_cols = jnp.minimum(tile_cols, (highest_row - col_ids) // N_COL)
    column = col_ids + N_COL * tile_cols
    least_depth = jnp.maximum(column - owners + N_ROW - 1, 0) // N_ROW
    depth = jax.random.randint(jax.random.fold_in(base_key, 2), (N_ROW, N_COL, CHILD), least_depth, ROW_TILES)
    tile_rows = owners + N_ROW * depth
    counts = jax.random.randint(jax.random.fold_in(base_key, 4), (N_ROW, N_COL), CHILD // 2, CHILD + 1)
    counts = counts.at[:, 0].set(CHILD)
    return (tile_rows, tile_cols, counts)


def draw_child_rows(key, part):
    return child_layout(key)[0]


def draw_child_cols(key, part):
    return child_layout(key)[1]


def draw_child_counts(key, part):
    return child_layout(key)[2]


def draw_front_panels(key, part):
    shape = (ROW_TILES, N_ROW, TILE, COL_TILES, N_COL, TILE)
    values = 0.25 * jax.random.normal(key, shape, jnp.float32)
    row_index = (lax.broadcasted_iota(jnp.int32, shape, 0) * N_ROW + lax.broadcasted_iota(jnp.int32, shape, 1)) * TILE + lax.broadcasted_iota(jnp.int32, shape, 2)
    col_index = (lax.broadcasted_iota(jnp.int32, shape, 3) * N_COL + lax.broadcasted_iota(jnp.int32, shape, 4)) * TILE + lax.broadcasted_iota(jnp.int32, shape, 5)
    return values + jnp.where(row_index == col_index, 32.0, 0.0)


def level_of(key, shape, split, low, largest):
    loudness, own = 1.0, jax.random.fold_in(key, 6)
    for position, blocks in split:
        heights = jnp.exp(jax.random.uniform(jax.random.fold_in(own, position), (blocks,), jnp.float32, low / len(split), largest / len(split)))
        loudness = loudness * jnp.repeat(heights, shape[position] // blocks).reshape([-1 if axis == position else 1 for axis in range(len(shape))])
    return loudness


def centred(own_key, dims, width, most, split=(), kind=jnp.bfloat16):
    entries = width * jax.random.normal(own_key, dims, jnp.float32)
    if split:
        entries = entries * level_of(own_key, dims, split, -0.22, 0.18)
    return jnp.clip(entries, -most, most).astype(kind)


def setup_inputs(seed: int = 0) -> dict:
    streams_of = jax.random.split(jax.random.key(seed), 8)
    return {
        "front_panels": draw_front_panels(jax.random.fold_in(streams_of[7], 71), 0),
        "child_update_tiles": centred(streams_of[1], (N_ROW, N_COL, CHILD, TILE, TILE), 0.25, 2.0, ((0, 4), (1, 8)), jnp.float32),
        "child_rows": draw_child_rows(jax.random.fold_in(streams_of[7], 71), 0),
        "child_cols": draw_child_cols(jax.random.fold_in(streams_of[7], 71), 0),
        "child_counts": draw_child_counts(jax.random.fold_in(streams_of[7], 71), 0),
        "row_maps": jax.vmap(lambda own: jax.random.permutation(own, TILE))(jax.random.split(streams_of[5], N_ROW * N_COL * CHILD)).reshape((N_ROW, N_COL, CHILD, TILE)).astype(jnp.int32),
        "col_maps": jax.vmap(lambda own: jax.random.permutation(own, TILE))(jax.random.split(streams_of[6], N_ROW * N_COL * CHILD)).reshape((N_ROW, N_COL, CHILD, TILE)).astype(jnp.int32),
    }


def permute_tile(inputs):
    block, row_map, col_map = inputs
    labels = lax.broadcasted_iota(jnp.int32, (TILE, TILE), 1)
    row_indicator = (row_map[:, None] == labels).astype(jnp.float32)
    column_indicator = (col_map[:, None] == labels).astype(jnp.float32)
    shifted_tiles = jnp.dot(row_indicator.T.astype(jnp.float32), block.astype(jnp.float32), precision=lax.Precision.HIGHEST, preferred_element_type=jnp.float32)
    return jnp.dot(shifted_tiles.astype(jnp.float32), column_indicator.astype(jnp.float32), precision=lax.Precision.HIGHEST, preferred_element_type=jnp.float32)

def reference(front_panels, child_update_tiles, child_rows, child_cols, child_counts, row_maps, col_maps):
    tile_count = FRONT // TILE
    total = N_ROW * N_COL * CHILD
    shifted_tiles = lax.map(permute_tile, (child_update_tiles.reshape(total, TILE, TILE), row_maps.reshape(total, TILE), col_maps.reshape(total, TILE)))
    slot_ids = lax.broadcasted_iota(jnp.int32, (N_ROW, N_COL, CHILD), 2)
    col_ids = lax.broadcasted_iota(jnp.int32, (N_ROW, N_COL, CHILD), 1)
    is_live = (slot_ids < child_counts[:, :, None]).astype(jnp.float32).reshape(total)
    shifted_tiles = shifted_tiles * is_live[:, None, None]
    target_rows = child_rows.reshape(total).astype(jnp.int32)
    target_cols = (col_ids + N_COL * child_cols).reshape(total).astype(jnp.int32)
    blocks = front_panels.reshape(tile_count, TILE, tile_count, TILE)
    blocks = blocks.at[target_rows, :, target_cols, :].add(shifted_tiles)
    matrix = blocks.reshape(FRONT, FRONT)
    tile_i = (jnp.arange(FRONT, dtype=jnp.int32) // TILE)[:, None]
    tile_j = (jnp.arange(FRONT, dtype=jnp.int32) // TILE)[None, :]
    lower = jnp.where(tile_i > tile_j, matrix, jnp.float32(0.0))
    diagonal = jnp.where(tile_i == tile_j, matrix, jnp.float32(0.0))
    matrix = lower + lower.T + 0.5 * (diagonal + diagonal.T)
    factor = jnp.linalg.cholesky(matrix[:TILE, :TILE])
    panel = jax.scipy.linalg.solve_triangular(factor, matrix[TILE:, :TILE].T, lower=True).T
    trailing = matrix[TILE:, TILE:] - jnp.dot(panel.astype(jnp.float32), panel.T.astype(jnp.float32), precision=lax.Precision.HIGHEST, preferred_element_type=jnp.float32)
    matrix = matrix.at[:TILE, :TILE].set(factor)
    matrix = matrix.at[TILE:, :TILE].set(panel)
    matrix = matrix.at[TILE:, TILE:].set(trailing)
    matrix = jnp.where(tile_i >= tile_j, matrix, jnp.float32(0.0))
    return matrix.reshape(ROW_TILES, N_ROW, TILE, COL_TILES, N_COL, TILE)
```

```python
import functools

import jax
import jax.numpy as jnp
from jax import lax
from jax.experimental import pallas as pl
from jax.experimental.pallas import tpu as pltpu
from jax.sharding import PartitionSpec as P

HIGHEST = lax.Precision.HIGHEST
LANES = 128
VMEM_LIMIT = 48 << 20


def dot_nt(left, right):
    return lax.dot_general(
        left,
        right,
        (((1,), (1,)), ((), ())),
        precision=HIGHEST,
        preferred_element_type=jnp.float32,
    )


def depth_blocks(a, row_size, col_size):
    return (a * row_size + row_size - 1) // col_size + 1


def move_kernel(
    row_size, capacity, ids_ref, rows_ref, count_ref, tiles_ref, row_map_ref, col_map_ref, *out_refs
):
    slots, width = tiles_ref.shape[0], tiles_ref.shape[1]
    labels = lax.broadcasted_iota(jnp.int32, (width, width), 0)
    count = count_ref[0]

    def one(owner, place, out_ref):
        def scan(k, state):
            chosen, seen = state
            hit = (lax.rem(rows_ref[k], row_size) == owner) & (k < count)
            chosen = jnp.where(hit & (seen == place), k, chosen)
            return chosen, seen + hit.astype(jnp.int32)

        chosen, _ = lax.fori_loop(0, slots, scan, (jnp.int32(0), jnp.int32(0)))
        row_hot = (labels == row_map_ref[chosen]).astype(jnp.float32)
        col_hot = (labels == col_map_ref[chosen]).astype(jnp.float32)
        shifted = jnp.dot(
            row_hot, tiles_ref[chosen], precision=HIGHEST, preferred_element_type=jnp.float32
        )
        out_ref[place] = dot_nt(shifted, col_hot)

    for shift, out_ref in enumerate(out_refs):
        owner = lax.rem(ids_ref[0] + shift, row_size)
        for place in range(capacity):
            one(owner, place, out_ref)


def move_tiles(row_size, capacity, ids, rows, count, tiles, row_maps, col_maps):
    slots, width = tiles.shape[0], tiles.shape[1]
    smem = pl.BlockSpec(memory_space=pltpu.SMEM)
    vmem = pl.BlockSpec(memory_space=pltpu.VMEM)
    return pl.pallas_call(
        functools.partial(move_kernel, row_size, capacity),
        out_shape=[jax.ShapeDtypeStruct((capacity, width, width), jnp.float32)] * row_size,
        in_specs=[smem, smem, smem, vmem, vmem, vmem],
        out_specs=[vmem] * row_size,
        compiler_params=pltpu.CompilerParams(vmem_limit_bytes=VMEM_LIMIT),
        name="move_tiles",
    )(ids, rows, count, tiles, row_maps.reshape(slots, 1, width), col_maps.reshape(slots, 1, width))


def locate_kernel(row_size, col_size, capacity, slots, ids_ref, meta_ref, own_ref, lead_ref):
    my_row, my_col = ids_ref[0], ids_ref[1]
    for table, col in ((own_ref, my_col), (lead_ref, 0)):

        def clear(n, carry):
            table[0, n] = -1
            table[1, n] = -1
            return carry

        lax.fori_loop(0, row_size * capacity, clear, 0)

        def source(s, carry):
            line = lax.rem(my_row + row_size - s, row_size) * col_size + col
            count = meta_ref[line, 2 * slots]

            def slot(k, seen):
                target = meta_ref[line, k]
                hit = (lax.rem(target, row_size) == my_row) & (k < count)

                @pl.when(hit)
                def _():
                    table[0, s * capacity + seen] = target // row_size
                    table[1, s * capacity + seen] = meta_ref[line, slots + k]

                return jnp.minimum(seen + hit.astype(jnp.int32), capacity - 1)

            lax.fori_loop(0, slots, slot, jnp.int32(0))
            return carry

        lax.fori_loop(0, row_size, source, 0)


def locate(row_size, col_size, capacity, slots, ids, meta):
    smem = pl.BlockSpec(memory_space=pltpu.SMEM)
    shape = jax.ShapeDtypeStruct((2, row_size * capacity), jnp.int32)
    return pl.pallas_call(
        functools.partial(locate_kernel, row_size, col_size, capacity, slots),
        out_shape=(shape, shape),
        in_specs=[smem, smem],
        out_specs=(smem, smem),
        name="locate",
    )(ids, meta)


def lead_kernel(ids_ref, lead_ref, own_ref, kids_ref, out_ref, corner_ref):
    out_ref[...] = own_ref[...]
    chunk = own_ref.shape[1]
    for n in range(kids_ref.shape[0]):

        @pl.when((lead_ref[0, n] >= 0) & (lead_ref[1, n] == 0))
        def _():
            out_ref[lead_ref[0, n]] += kids_ref[n]

    corner_ref[...] = jnp.zeros_like(corner_ref)

    @pl.when(ids_ref[0] == 0)
    def _():
        start = pl.multiple_of(ids_ref[1] * chunk, chunk)
        corner_ref[pl.ds(start, chunk), :] = out_ref[0]


def lead_rows(ids, lead, own, kids):
    smem = pl.BlockSpec(memory_space=pltpu.SMEM)
    vmem = pl.BlockSpec(memory_space=pltpu.VMEM)
    width = own.shape[2]
    return pl.pallas_call(
        lead_kernel,
        out_shape=(
            jax.ShapeDtypeStruct(own.shape, jnp.float32),
            jax.ShapeDtypeStruct((width, width), jnp.float32),
        ),
        in_specs=[smem, smem, vmem, vmem],
        out_specs=(vmem, vmem),
        compiler_params=pltpu.CompilerParams(vmem_limit_bytes=VMEM_LIMIT),
        name="lead_rows",
    )(ids, lead, own, kids)


def panel_kernel(ids_ref, inverse_ref, factor_ref, rows_ref, cols_ref, row_out, col_out):
    width = inverse_ref.shape[0]
    inverse = inverse_ref[...]

    def row(a, carry):
        row_out[a] = dot_nt(rows_ref[:, a].reshape(width, width), inverse)
        return carry

    lax.fori_loop(0, row_out.shape[0], row, 0)

    @pl.when(ids_ref[0] == 0)
    def _():
        row_out[0] = factor_ref[...]

    def col(b, carry):
        col_out[b] = dot_nt(cols_ref[:, b].reshape(width, width), inverse)
        return carry

    lax.fori_loop(0, col_out.shape[0], col, 0)


def panels(ids, inverse, factor, rows, cols):
    smem = pl.BlockSpec(memory_space=pltpu.SMEM)
    vmem = pl.BlockSpec(memory_space=pltpu.VMEM)
    width = inverse.shape[0]
    return pl.pallas_call(
        panel_kernel,
        out_shape=(
            jax.ShapeDtypeStruct((rows.shape[1], width, width), jnp.float32),
            jax.ShapeDtypeStruct((cols.shape[1], width, width), jnp.float32),
        ),
        in_specs=[smem, vmem, vmem, vmem, vmem],
        out_specs=(vmem, vmem),
        compiler_params=pltpu.CompilerParams(vmem_limit_bytes=VMEM_LIMIT),
        name="panels",
    )(ids, inverse, factor, rows, cols)


def pack_kernel(depths, counts, front_ref, out_ref, in_buf, out_buf, in_sem, out_sem):
    col_size = front_ref.shape[4]
    chunk = front_ref.shape[2]

    def fetch(i):
        a, nb, slot = depths[i], counts[i], i % 2
        return [
            pltpu.make_async_copy(
                front_ref.at[a, 0, :, pl.ds(0, nb), :, pl.ds(half * LANES, LANES)],
                in_buf.at[slot, half, :, pl.ds(0, nb)],
                in_sem.at[slot, half],
            )
            for half in range(2)
        ]

    def send(i):
        first, nb, slot = sum(counts[:i]), counts[i], i % 2
        return pltpu.make_async_copy(
            out_buf.at[slot, :, pl.ds(0, nb)], out_ref.at[:, pl.ds(first, nb)], out_sem.at[slot]
        )

    steps = len(depths)
    for copy in fetch(0):
        copy.start()
    for i in range(steps):
        slot, nb = i % 2, counts[i]
        if i + 1 < steps:
            for copy in fetch(i + 1):
                copy.start()
        for copy in fetch(i):
            copy.wait()
        if i >= 2:
            send(i - 2).wait()
        for half in range(2):
            total = in_buf.shape[3]
            flat = in_buf.at[slot, half].reshape(chunk * total * col_size, LANES)
            for b in range(nb):
                for c in range(col_size):
                    out_buf[slot, c, b, :, half * LANES : (half + 1) * LANES] = flat[
                        pl.ds(b * col_size + c, chunk, stride=total * col_size), :
                    ]
        send(i).start()
    for i in range(max(steps - 2, 0), steps):
        send(i).wait()


def pack(front, depths, counts):
    chunk, col_size, width = front.shape[2], front.shape[4], front.shape[5]
    most = max(counts)
    return pl.pallas_call(
        functools.partial(pack_kernel, depths, counts),
        out_shape=jax.ShapeDtypeStruct((col_size, sum(counts), chunk, width), jnp.float32),
        in_specs=[pl.BlockSpec(memory_space=pltpu.HBM)],
        out_specs=pl.BlockSpec(memory_space=pltpu.HBM),
        scratch_shapes=[
            pltpu.VMEM((2, 2, chunk, most, col_size, LANES), jnp.float32),
            pltpu.VMEM((2, col_size, most, chunk, width), jnp.float32),
            pltpu.SemaphoreType.DMA((2, 2)),
            pltpu.SemaphoreType.DMA((2,)),
        ],
        compiler_params=pltpu.CompilerParams(vmem_limit_bytes=VMEM_LIMIT),
        name="pack",
    )(front)


def finish_kernel(
    depths,
    counts,
    row_size,
    col_size,
    ids_ref,
    own_ref,
    recv_ref,
    rows_ref,
    cols_ref,
    kids_ref,
    *rest,
):
    out_ref, in_buf, row_buf, out_buf, in_sem, row_sem, out_sem = rest[-7:]
    my_row, my_col = ids_ref[0], ids_ref[1]
    width = cols_ref.shape[1]
    chunk = width // col_size
    halves = width // LANES
    blocks = cols_ref.shape[0]
    stride = blocks * halves

    def fetch(i):
        a, nb, slot, first = depths[i], counts[i], i % 2, sum(counts[:i])
        return (
            pltpu.make_async_copy(
                recv_ref.at[:, pl.ds(first, nb)], in_buf.at[slot, :, pl.ds(0, nb)], in_sem.at[slot]
            ),
            pltpu.make_async_copy(rows_ref.at[a], row_buf.at[slot], row_sem.at[slot]),
        )

    def send(i):
        return pltpu.make_async_copy(out_buf.at[i % 2], out_ref.at[depths[i]], out_sem.at[i % 2])

    steps = len(depths)
    for copy in fetch(0):
        copy.start()
    for i in range(steps):
        a, nb, slot = depths[i], counts[i], i % 2
        if i + 1 < steps:
            for copy in fetch(i + 1):
                copy.start()
        for copy in fetch(i):
            copy.wait()
        if i >= 2:
            send(i - 2).wait()
        for n in range(kids_ref.shape[0]):

            @pl.when(own_ref[0, n] == a)
            def _():
                b = own_ref[1, n]
                in_buf[slot, :, b] += kids_ref[n].reshape(col_size, chunk, width)

        tile_i = a * row_size + my_row

        def store(b, tile):
            for half in range(halves):
                out_buf[slot, pl.ds(b * halves + half, width, stride=stride), :] = tile[
                    :, half * LANES : (half + 1) * LANES
                ]

        def update(b):
            return dot_nt(row_buf[slot], cols_ref[b])

        for b in range(nb):
            tile = in_buf[slot, :, b].reshape(width, width)
            tile_j = b * col_size + my_col
            if b < nb - 1:
                store(b, tile - update(b))
            else:

                @pl.when(tile_i > tile_j)
                def _():
                    store(b, tile - update(b))

                @pl.when(tile_i == tile_j)
                def _():
                    store(b, 0.5 * (tile + tile.T) - update(b))

                @pl.when(tile_i < tile_j)
                def _():
                    store(b, jnp.zeros_like(tile))

        @pl.when(my_col == 0)
        def _():
            store(0, row_buf[slot])

        zero = jnp.zeros((width, LANES), jnp.float32)
        for n in range(nb * halves, stride):
            out_buf[slot, pl.ds(n, width, stride=stride), :] = zero
        send(i).start()
    for i in range(max(steps - 2, 0), steps):
        send(i).wait()


def finish(depths, counts, row_size, col_size, ids, own, recv, rows, cols, kids, out=None):
    smem = pl.BlockSpec(memory_space=pltpu.SMEM)
    vmem = pl.BlockSpec(memory_space=pltpu.VMEM)
    hbm = pl.BlockSpec(memory_space=pltpu.HBM)
    blocks, width = cols.shape[0], cols.shape[1]
    chunk = width // col_size
    lines = width * blocks * (width // LANES)
    operands = [ids, own, recv, rows, cols, kids]
    in_specs = [smem, smem, hbm, hbm, vmem, vmem]
    aliases = {}
    if out is not None:
        operands.append(out)
        in_specs.append(hbm)
        aliases = {6: 0}
    return pl.pallas_call(
        functools.partial(finish_kernel, depths, counts, row_size, col_size),
        out_shape=jax.ShapeDtypeStruct((rows.shape[0], lines, LANES), jnp.float32),
        in_specs=in_specs,
        out_specs=hbm,
        scratch_shapes=[
            pltpu.VMEM((2, col_size, max(counts), chunk, width), jnp.float32),
            pltpu.VMEM((2, width, width), jnp.float32),
            pltpu.VMEM((2, lines, LANES), jnp.float32),
            pltpu.SemaphoreType.DMA((2,)),
            pltpu.SemaphoreType.DMA((2,)),
            pltpu.SemaphoreType.DMA((2,)),
        ],
        input_output_aliases=aliases,
        compiler_params=pltpu.CompilerParams(vmem_limit_bytes=VMEM_LIMIT),
        name="finish",
    )(*operands)


def on_device(front, child_tiles, child_rows, child_cols, child_counts, row_maps, col_maps):
    row_size, col_size = lax.axis_size("row"), lax.axis_size("col")
    my_row, my_col = lax.axis_index("row"), lax.axis_index("col")
    row_tiles, chunk, col_tiles, width = front.shape[0], front.shape[2], front.shape[3], front.shape[5]
    slots = child_tiles.shape[2]
    capacity = slots // 4
    arrivals = row_size * capacity
    group = col_size // row_size
    ids = jnp.stack([my_row, my_col]).astype(jnp.int32)

    counts = [depth_blocks(a, row_size, col_size) for a in range(row_tiles)]
    split = row_tiles // 2
    parts = [list(range(row_tiles - 1, split - 1, -1)), list(range(split - 1, -1, -1))]

    packed = [pack(front, part, [counts[a] for a in part]) for part in parts]
    first = lax.all_to_all(packed[0], "col", split_axis=0, concat_axis=0, tiled=True)

    child_tiles, _ = lax.optimization_barrier((child_tiles, packed[0]))
    moved = move_tiles(
        row_size,
        capacity,
        ids,
        child_rows.reshape(slots),
        child_counts.reshape(1),
        child_tiles.reshape(slots, width, width),
        row_maps.reshape(slots, width),
        col_maps.reshape(slots, width),
    )
    meta = jnp.concatenate(
        [child_rows.reshape(1, slots), child_cols.reshape(1, slots), child_counts.reshape(1, 1)], axis=1
    )
    meta = lax.all_gather(meta, ("row", "col"), axis=0, tiled=True)
    own, lead = locate(row_size, col_size, capacity, slots, ids, meta)

    kids = jnp.concatenate(
        [moved[0]]
        + [
            lax.ppermute(moved[shift], "row", [(r, (r + shift) % row_size) for r in range(row_size)])
            for shift in range(1, row_size)
        ]
    )

    pieces = kids.reshape(arrivals, col_size, chunk, width)
    lead_kids = jnp.where(my_col == 0, pieces[:, 0], 0.0)
    for c in range(1, col_size):
        lead_kids = lead_kids + lax.ppermute(pieces[:, c], "col", [(0, c)])
    raw, corner = lead_rows(ids, lead, front[:, 0, :, 0, 0, :], lead_kids)

    corner = lax.psum(corner, ("row", "col"))
    corner = 0.5 * (corner + corner.T)
    factor = jnp.linalg.cholesky(corner)
    inverse = jax.scipy.linalg.solve_triangular(
        factor, jnp.eye(width, dtype=jnp.float32), lower=True
    )

    raw_rows = lax.all_gather(raw, "col", axis=0, tiled=False)
    mine = lax.dynamic_index_in_dim(
        raw_rows.reshape(col_size, col_tiles, group, chunk, width),
        my_col // row_size,
        2,
        keepdims=False,
    )
    raw_cols = jnp.where(my_row == my_col % row_size, mine, 0.0)
    for shift in range(1, row_size):
        pairs = [
            ((c % row_size) * col_size + c, ((c + shift) % row_size) * col_size + c)
            for c in range(col_size)
        ]
        raw_cols = raw_cols + lax.ppermute(mine, ("row", "col"), pairs)
    rows, cols = panels(ids, inverse, factor, raw_rows, raw_cols)

    later, rows, cols = lax.optimization_barrier((packed[1], rows, cols))
    second = lax.all_to_all(later, "col", split_axis=0, concat_axis=0, tiled=True)

    out = None
    for part, recv in zip(parts, (first, second)):
        out = finish(
            part, [counts[a] for a in part], row_size, col_size, ids, own, recv, rows, cols, kids, out
        )
    return out.reshape(row_tiles, 1, width, col_tiles, 1, width)


def solution(mesh):
    return jax.shard_map(
        on_device,
        mesh=mesh,
        in_specs=(
            P(None, "row", "col", None, None, None),
            P("row", "col", None, None, None),
            P("row", "col", None),
            P("row", "col", None),
            P("row", "col"),
            P("row", "col", None, None),
            P("row", "col", None, None),
        ),
        out_specs=P(None, "row", None, None, "col", None),
        check_vma=False,
    )
```

```python
import functools

import jax
import jax.numpy as jnp
from jax import lax
from jax.experimental import pallas as pl
from jax.experimental.pallas import tpu as pltpu
from jax.sharding import PartitionSpec as P

HIGHEST = lax.Precision.HIGHEST
LANES = 128
VMEM_LIMIT = 60 << 20


def dot_nt(left, right):
    return lax.dot_general(
        left,
        right,
        (((1,), (1,)), ((), ())),
        precision=HIGHEST,
        preferred_element_type=jnp.float32,
    )


def bf16_nt(left, right):
    return lax.dot_general(
        left, right, (((1,), (1,)), ((), ())), preferred_element_type=jnp.float32
    )


def depth_blocks(a, row_size, col_size):
    return (a * row_size + row_size - 1) // col_size + 1


def move_kernel(
    row_size,
    capacity,
    ids_ref,
    rows_ref,
    cols_ref,
    count_ref,
    tiles_ref,
    row_map_ref,
    col_map_ref,
    *out_refs,
):
    slots, width = tiles_ref.shape[0], tiles_ref.shape[1]
    out_refs, lead_refs = out_refs[:row_size], out_refs[row_size:]
    chunk = width // len(lead_refs)
    labels = lax.broadcasted_iota(jnp.int32, (width, width), 0)
    count = count_ref[0]

    def one(shift, place, out_ref):
        owner = lax.rem(ids_ref[0] + shift, row_size)
        def scan(k, state):
            chosen, seen = state
            hit = (lax.rem(rows_ref[k], row_size) == owner) & (k < count)
            chosen = jnp.where(hit & (seen == place), k, chosen)
            return chosen, seen + hit.astype(jnp.int32)

        chosen, seen = lax.fori_loop(0, slots, scan, (jnp.int32(0), jnp.int32(0)))
        row_hot = (labels == row_map_ref[chosen]).astype(jnp.float32)
        col_hot = (labels == col_map_ref[chosen]).astype(jnp.float32)
        shifted = jnp.dot(
            row_hot, tiles_ref[chosen], precision=HIGHEST, preferred_element_type=jnp.float32
        )
        tile = dot_nt(shifted, col_hot)
        out_ref[place] = tile
        here = (seen > place) & (cols_ref[chosen] == 0)
        target = jnp.where(here, rows_ref[chosen] // row_size, -1).astype(jnp.float32)
        for c, lead_ref in enumerate(lead_refs):
            lead_ref[shift, pl.ds(place * chunk, chunk), :] = tile[c * chunk : (c + 1) * chunk]
            lead_ref[shift, pl.ds(capacity * chunk + place * 8, 8), :] = jnp.full(
                (8, width), target
            )

    for shift, out_ref in enumerate(out_refs):
        for place in range(capacity):
            one(shift, place, out_ref)


def move_tiles(row_size, col_size, capacity, ids, rows, cols, count, tiles, row_maps, col_maps):
    slots, width = tiles.shape[0], tiles.shape[1]
    smem = pl.BlockSpec(memory_space=pltpu.SMEM)
    vmem = pl.BlockSpec(memory_space=pltpu.VMEM)
    return pl.pallas_call(
        functools.partial(move_kernel, row_size, capacity),
        out_shape=[jax.ShapeDtypeStruct((capacity, width, width), jnp.float32)] * row_size
        + [
            jax.ShapeDtypeStruct((row_size, capacity * (width // col_size + 8), width), jnp.float32)
        ]
        * col_size,
        in_specs=[smem, smem, smem, smem, vmem, vmem, vmem],
        out_specs=[vmem] * (row_size + col_size),
        compiler_params=pltpu.CompilerParams(vmem_limit_bytes=VMEM_LIMIT),
        name="move_tiles",
    )(ids, rows, cols, count, tiles, row_maps.reshape(slots, 1, width), col_maps.reshape(slots, 1, width))


def locate_kernel(row_size, capacity, slots, ids_ref, meta_ref, own_ref):
    my_row = ids_ref[0]

    def clear(n, carry):
        own_ref[0, n] = -1
        own_ref[1, n] = -1
        return carry

    lax.fori_loop(0, row_size * capacity, clear, 0)

    def source(s, carry):
        line = lax.rem(my_row + row_size - s, row_size)
        count = meta_ref[line, 2 * slots]

        def slot(k, seen):
            target = meta_ref[line, k]
            hit = (lax.rem(target, row_size) == my_row) & (k < count)

            @pl.when(hit)
            def _():
                own_ref[0, s * capacity + seen] = target // row_size
                own_ref[1, s * capacity + seen] = meta_ref[line, slots + k]

            return jnp.minimum(seen + hit.astype(jnp.int32), capacity - 1)

        lax.fori_loop(0, slots, slot, jnp.int32(0))
        return carry

    lax.fori_loop(0, row_size, source, 0)


def locate(row_size, capacity, slots, ids, meta):
    smem = pl.BlockSpec(memory_space=pltpu.SMEM)
    return pl.pallas_call(
        functools.partial(locate_kernel, row_size, capacity, slots),
        out_shape=jax.ShapeDtypeStruct((2, row_size * capacity), jnp.int32),
        in_specs=[smem, smem],
        out_specs=smem,
        name="locate",
    )(ids, meta)


def lead_kernel(capacity, front_ref, *refs):
    kids_refs, (out_ref, buf, sem) = refs[:-3], refs[-3:]
    row_tiles, chunk, col_size = front_ref.shape[0], front_ref.shape[2], front_ref.shape[4]
    copies = [
        pltpu.make_async_copy(
            front_ref.at[:, 0, :, 0, :, pl.ds(half * LANES, LANES)], buf.at[half], sem.at[half]
        )
        for half in range(2)
    ]
    for copy in copies:
        copy.start()
    for copy in copies:
        copy.wait()
    for half in range(2):
        flat = buf.at[half].reshape(row_tiles * chunk * col_size, LANES)
        for a in range(row_tiles):
            out_ref[a, :, half * LANES : (half + 1) * LANES] = flat[
                pl.ds(a * chunk * col_size, chunk, stride=col_size), :
            ]
    for kids_ref in kids_refs:
        for place in range(capacity):
            kid = kids_ref[pl.ds(place * chunk, chunk), :]
            target = kids_ref[pl.ds(capacity * chunk + place * 8, 1), :]
            for a in range(row_tiles):
                out_ref[a] += jnp.where(target == a, kid, 0.0)


def lead_rows(capacity, front, kids):
    vmem = pl.BlockSpec(memory_space=pltpu.VMEM)
    row_tiles, chunk, col_size, width = front.shape[0], front.shape[2], front.shape[4], front.shape[5]
    return pl.pallas_call(
        functools.partial(lead_kernel, capacity),
        out_shape=jax.ShapeDtypeStruct((row_tiles, chunk, width), jnp.float32),
        in_specs=[pl.BlockSpec(memory_space=pltpu.HBM)] + [vmem] * len(kids),
        out_specs=vmem,
        scratch_shapes=[
            pltpu.VMEM((2, row_tiles, chunk, col_size, LANES), jnp.float32),
            pltpu.SemaphoreType.DMA((2,)),
        ],
        compiler_params=pltpu.CompilerParams(vmem_limit_bytes=VMEM_LIMIT),
        name="lead_rows",
    )(front, *kids)


def order_kernel(ids_ref, *refs):
    same, other_ref, out_ref = refs[:-2], refs[-2], refs[-1]
    for k, same_ref in enumerate(same):
        out_ref[lax.bitwise_xor(ids_ref[1], 2 * k)] = same_ref[...]
        out_ref[lax.bitwise_xor(ids_ref[1], 2 * k + 1)] = other_ref[k]


def order_rows(ids, same, other):
    smem = pl.BlockSpec(memory_space=pltpu.SMEM)
    vmem = pl.BlockSpec(memory_space=pltpu.VMEM)
    return pl.pallas_call(
        order_kernel,
        out_shape=jax.ShapeDtypeStruct((2 * len(same),) + same[0].shape, jnp.float32),
        in_specs=[smem] + [vmem] * (1 + len(same)),
        out_specs=vmem,
        compiler_params=pltpu.CompilerParams(vmem_limit_bytes=VMEM_LIMIT),
        name="order_rows",
    )(ids, *same, other)


def halves_of(value):
    high = value.astype(jnp.bfloat16)
    return high, (value - high.astype(jnp.float32)).astype(jnp.bfloat16)


def panel_kernel(ids_ref, inverse_ref, factor_ref, rows_ref, cols_ref, row_out, high_out, low_out):
    width = inverse_ref.shape[0]
    inverse = inverse_ref[...]

    def row(a, carry):
        row_out[a] = dot_nt(rows_ref[:, a].reshape(width, width), inverse)
        return carry

    lax.fori_loop(0, row_out.shape[0], row, 0)

    @pl.when(ids_ref[0] == 0)
    def _():
        row_out[0] = factor_ref[...]

    def column(b, carry):
        col = dot_nt(cols_ref[:, b].reshape(width, width), inverse)
        high_out[b], low_out[b] = halves_of(col)
        return carry

    lax.fori_loop(0, high_out.shape[0], column, 0)


def panels(ids, inverse, factor, rows, cols):
    smem = pl.BlockSpec(memory_space=pltpu.SMEM)
    vmem = pl.BlockSpec(memory_space=pltpu.VMEM)
    width = inverse.shape[0]
    return pl.pallas_call(
        panel_kernel,
        out_shape=(
            jax.ShapeDtypeStruct((rows.shape[1], width, width), jnp.float32),
            jax.ShapeDtypeStruct((cols.shape[1], width, width), jnp.bfloat16),
            jax.ShapeDtypeStruct((cols.shape[1], width, width), jnp.bfloat16),
        ),
        in_specs=[smem, vmem, vmem, vmem, vmem],
        out_specs=(vmem, vmem, vmem),
        compiler_params=pltpu.CompilerParams(vmem_limit_bytes=VMEM_LIMIT),
        name="panels",
    )(ids, inverse, factor, rows, cols)


def pack_kernel(depths, counts, front_ref, out_ref, in_buf, out_buf, in_sem, out_sem):
    col_size = front_ref.shape[4]
    chunk = front_ref.shape[2]

    def fetch(i):
        a, nb, slot = depths[i], counts[i], i % 2
        return [
            pltpu.make_async_copy(
                front_ref.at[a, 0, :, pl.ds(0, nb), :, pl.ds(half * LANES, LANES)],
                in_buf.at[slot, half, :, pl.ds(0, nb)],
                in_sem.at[slot, half],
            )
            for half in range(2)
        ]

    def send(i):
        first, nb, slot = sum(counts[:i]), counts[i], i % 2
        return pltpu.make_async_copy(
            out_buf.at[slot, :, pl.ds(0, nb)], out_ref.at[:, pl.ds(first, nb)], out_sem.at[slot]
        )

    steps = len(depths)
    for copy in fetch(0):
        copy.start()
    for i in range(steps):
        slot, nb = i % 2, counts[i]
        if i + 1 < steps:
            for copy in fetch(i + 1):
                copy.start()
        for copy in fetch(i):
            copy.wait()
        if i >= 2:
            send(i - 2).wait()
        for half in range(2):
            total = in_buf.shape[3]
            flat = in_buf.at[slot, half].reshape(chunk * total * col_size, LANES)
            for b in range(nb):
                for c in range(col_size):
                    out_buf[slot, c, b, :, half * LANES : (half + 1) * LANES] = flat[
                        pl.ds(b * col_size + c, chunk, stride=total * col_size), :
                    ]
        send(i).start()
    for i in range(max(steps - 2, 0), steps):
        send(i).wait()


def pack(front, depths, counts):
    chunk, col_size, width = front.shape[2], front.shape[4], front.shape[5]
    most = max(counts)
    return pl.pallas_call(
        functools.partial(pack_kernel, depths, counts),
        out_shape=jax.ShapeDtypeStruct((col_size, sum(counts), chunk, width), jnp.float32),
        in_specs=[pl.BlockSpec(memory_space=pltpu.HBM)],
        out_specs=pl.BlockSpec(memory_space=pltpu.HBM),
        scratch_shapes=[
            pltpu.VMEM((2, 2, chunk, most, col_size, LANES), jnp.float32),
            pltpu.VMEM((2, col_size, most, chunk, width), jnp.float32),
            pltpu.SemaphoreType.DMA((2, 2)),
            pltpu.SemaphoreType.DMA((2,)),
        ],
        compiler_params=pltpu.CompilerParams(vmem_limit_bytes=VMEM_LIMIT),
        name="pack",
    )(front)


def finish_kernel(
    depths,
    counts,
    row_size,
    col_size,
    ids_ref,
    own_ref,
    recv_ref,
    rows_ref,
    high_ref,
    low_ref,
    kids_ref,
    *rest,
):
    out_ref, in_buf, row_buf, out_buf, in_sem, row_sem, out_sem = rest[-7:]
    my_row, my_col = ids_ref[0], ids_ref[1]
    width = high_ref.shape[1]
    chunk = width // col_size
    halves = width // LANES
    blocks = high_ref.shape[0]
    stride = blocks * halves

    def fetch(i):
        a, nb, slot, first = depths[i], counts[i], i % 2, sum(counts[:i])
        return (
            pltpu.make_async_copy(
                recv_ref.at[:, pl.ds(first, nb)], in_buf.at[slot, :, pl.ds(0, nb)], in_sem.at[slot]
            ),
            pltpu.make_async_copy(rows_ref.at[a], row_buf.at[slot], row_sem.at[slot]),
        )

    def send(i):
        return pltpu.make_async_copy(out_buf.at[i % 2], out_ref.at[depths[i]], out_sem.at[i % 2])

    steps = len(depths)
    for copy in fetch(0):
        copy.start()
    for i in range(steps):
        a, nb, slot = depths[i], counts[i], i % 2
        if i + 1 < steps:
            for copy in fetch(i + 1):
                copy.start()
        for copy in fetch(i):
            copy.wait()
        if i >= 2:
            send(i - 2).wait()
        for n in range(kids_ref.shape[0]):

            @pl.when(own_ref[0, n] == a)
            def _():
                b = own_ref[1, n]
                in_buf[slot, :, b] += kids_ref[n].reshape(col_size, chunk, width)

        tile_i = a * row_size + my_row

        def store(b, tile):
            for half in range(halves):
                out_buf[slot, pl.ds(b * halves + half, width, stride=stride), :] = tile[
                    :, half * LANES : (half + 1) * LANES
                ]

        row_high, row_low = halves_of(row_buf[slot])

        def update(b):
            return bf16_nt(row_high, high_ref[b]) + (
                bf16_nt(row_high, low_ref[b]) + bf16_nt(row_low, high_ref[b])
            )

        for b in range(nb):
            tile = in_buf[slot, :, b].reshape(width, width)
            tile_j = b * col_size + my_col
            if b < nb - 1:
                store(b, tile - update(b))
            else:

                @pl.when(tile_i > tile_j)
                def _():
                    store(b, tile - update(b))

                @pl.when(tile_i == tile_j)
                def _():
                    store(b, 0.5 * (tile + tile.T) - update(b))

                @pl.when(tile_i < tile_j)
                def _():
                    store(b, jnp.zeros_like(tile))

        @pl.when(my_col == 0)
        def _():
            store(0, row_buf[slot])

        zero = jnp.zeros((width, LANES), jnp.float32)
        for n in range(nb * halves, stride):
            out_buf[slot, pl.ds(n, width, stride=stride), :] = zero
        send(i).start()
    for i in range(max(steps - 2, 0), steps):
        send(i).wait()


def finish(depths, counts, row_size, col_size, ids, own, recv, rows, high, low, kids, out=None):
    smem = pl.BlockSpec(memory_space=pltpu.SMEM)
    vmem = pl.BlockSpec(memory_space=pltpu.VMEM)
    hbm = pl.BlockSpec(memory_space=pltpu.HBM)
    blocks, width = high.shape[0], high.shape[1]
    chunk = width // col_size
    lines = width * blocks * (width // LANES)
    operands = [ids, own, recv, rows, high, low, kids]
    in_specs = [smem, smem, hbm, hbm, vmem, vmem, vmem]
    aliases = {}
    if out is not None:
        operands.append(out)
        in_specs.append(hbm)
        aliases = {7: 0}
    return pl.pallas_call(
        functools.partial(finish_kernel, depths, counts, row_size, col_size),
        out_shape=jax.ShapeDtypeStruct((rows.shape[0], lines, LANES), jnp.float32),
        in_specs=in_specs,
        out_specs=hbm,
        scratch_shapes=[
            pltpu.VMEM((2, col_size, max(counts), chunk, width), jnp.float32),
            pltpu.VMEM((2, width, width), jnp.float32),
            pltpu.VMEM((2, lines, LANES), jnp.float32),
            pltpu.SemaphoreType.DMA((2,)),
            pltpu.SemaphoreType.DMA((2,)),
            pltpu.SemaphoreType.DMA((2,)),
        ],
        input_output_aliases=aliases,
        compiler_params=pltpu.CompilerParams(vmem_limit_bytes=VMEM_LIMIT),
        name="finish",
    )(*operands)


def on_device(front, child_tiles, child_rows, child_cols, child_counts, row_maps, col_maps):
    row_size, col_size = lax.axis_size("row"), lax.axis_size("col")
    my_row, my_col = lax.axis_index("row"), lax.axis_index("col")
    row_tiles, chunk, col_tiles, width = front.shape[0], front.shape[2], front.shape[3], front.shape[5]
    slots = child_tiles.shape[2]
    capacity = slots // 4
    arrivals = row_size * capacity
    group = col_size // row_size
    ids = jnp.stack([my_row, my_col]).astype(jnp.int32)

    counts = [depth_blocks(a, row_size, col_size) for a in range(row_tiles)]
    parts = [[row_tiles - 2], [row_tiles - 1, row_tiles - 3, row_tiles - 4]]
    last = (row_tiles - 5) * 3 // 4
    parts.append([a for a in range(row_tiles - 5, -1, -1) if a != last])
    parts.append([last])

    def exchange(part, *after):
        blocks = pack(front, part, [counts[a] for a in part])
        blocks = lax.optimization_barrier((blocks,) + after)[0]
        return lax.all_to_all(blocks, "col", split_axis=0, concat_axis=0, tiled=True)

    def along_row(shift):
        return [(r, (r + shift) % row_size) for r in range(row_size)]

    def across_col(k):
        return [(c, c ^ k) for c in range(col_size)]

    moved = move_tiles(
        row_size,
        col_size,
        capacity,
        ids,
        child_rows.reshape(slots),
        child_cols.reshape(slots),
        child_counts.reshape(1),
        child_tiles.reshape(slots, width, width),
        row_maps.reshape(slots, width),
        col_maps.reshape(slots, width),
    )
    moved, pieces = moved[:row_size], moved[row_size:]
    arrived = [exchange(parts[0], *moved)]

    lead = pieces[0]
    for c in range(1, col_size):
        lead = jnp.where(my_col == c, lax.ppermute(pieces[c], "col", [(0, c)]), lead)
    lead = [lead[0]] + [
        lax.ppermute(lead[shift], "row", along_row(shift)) for shift in range(1, row_size)
    ]
    raw = lead_rows(capacity, front, lead)

    raw, _ = lax.optimization_barrier((raw, arrived[0]))
    same = [raw] + [lax.ppermute(raw, "col", across_col(k)) for k in range(2, col_size, 2)]
    corner_half = jnp.stack([value[0] for value in same])
    corner_other = lax.ppermute(corner_half, "col", across_col(1))
    gathered = jnp.stack(same)
    arrived.append(exchange(parts[1], corner_other))
    other = lax.ppermute(gathered, "col", across_col(1))
    raw_rows = order_rows(ids, same, other)
    arrived.append(exchange(parts[2], arrived[1], other))

    meta = jnp.concatenate(
        [child_rows.reshape(1, slots), child_cols.reshape(1, slots), child_counts.reshape(1, 1)], axis=1
    )
    meta, _ = lax.optimization_barrier((meta, corner_other))
    meta = lax.all_gather(meta, "row", axis=0, tiled=True)
    own = locate(row_size, capacity, slots, ids, meta)
    *moved, _ = lax.optimization_barrier((*moved, corner_other))
    kids = jnp.concatenate(
        [moved[0]]
        + [lax.ppermute(moved[shift], "row", along_row(shift)) for shift in range(1, row_size)]
    )

    corner_mine = order_rows(
        ids, [corner_half[k : k + 1] for k in range(col_size // 2)], corner_other[:, None]
    ).reshape(width, width)
    corner = corner_mine
    corner = jnp.where(my_row == 0, corner, 0.0)
    for shift in range(1, row_size):
        corner = corner + lax.ppermute(corner_mine, "row", [(0, shift)])
    corner = 0.5 * (corner + corner.T)
    factor = jnp.linalg.cholesky(corner)
    inverse = jax.scipy.linalg.solve_triangular(
        factor, jnp.eye(width, dtype=jnp.float32), lower=True
    )

    mine = lax.dynamic_index_in_dim(
        raw_rows.reshape(col_size, col_tiles, group, chunk, width),
        my_col // row_size,
        2,
        keepdims=False,
    )
    raw_cols = jnp.where(my_row == my_col % row_size, mine, 0.0)
    for shift in range(1, row_size):
        steps = [
            ((c % row_size) * col_size + c, ((c + shift) % row_size) * col_size + c)
            for c in range(col_size)
        ]
        raw_cols = raw_cols + lax.ppermute(mine, ("row", "col"), steps)
    rows, high, low = panels(ids, inverse, factor, raw_rows, raw_cols)

    out = None
    for step, part in enumerate(parts):
        if step == 2:
            arrived.append(exchange(parts[3], arrived[2], out))
        out = finish(
            part,
            [counts[a] for a in part],
            row_size,
            col_size,
            ids,
            own,
            arrived[step],
            rows,
            high,
            low,
            kids,
            out,
        )
    return out.reshape(row_tiles, 1, width, col_tiles, 1, width)


def solution(mesh):
    return jax.shard_map(
        on_device,
        mesh=mesh,
        in_specs=(
            P(None, "row", "col", None, None, None),
            P("row", "col", None, None, None),
            P("row", "col", None),
            P("row", "col", None),
            P("row", "col"),
            P("row", "col", None, None),
            P("row", "col", None, None),
        ),
        out_specs=P(None, "row", None, None, "col", None),
        check_vma=False,
    )
```

```python
import functools

import jax
import jax.numpy as jnp
from jax import lax
from jax.experimental import pallas as pl
from jax.experimental.pallas import tpu as pltpu
from jax.sharding import PartitionSpec as P

HIGHEST = lax.Precision.HIGHEST
LANES = 128
VMEM_LIMIT = 60 << 20


def dot_nt(left, right):
    return lax.dot_general(
        left,
        right,
        (((1,), (1,)), ((), ())),
        precision=HIGHEST,
        preferred_element_type=jnp.float32,
    )


def bf16_nt(left, right):
    return lax.dot_general(
        left, right, (((1,), (1,)), ((), ())), preferred_element_type=jnp.float32
    )


def depth_blocks(a, row_size, col_size):
    return (a * row_size + row_size - 1) // col_size + 1


def shared_blocks(a, row_size, col_size):
    return (a * row_size + row_size - 1 - col_size // 2) // col_size + 1


def move_kernel(
    row_size,
    capacity,
    ids_ref,
    rows_ref,
    cols_ref,
    count_ref,
    tiles_ref,
    row_map_ref,
    col_map_ref,
    *out_refs,
):
    slots, width = tiles_ref.shape[0], tiles_ref.shape[1]
    out_refs, lead_refs = out_refs[:row_size], out_refs[row_size:]
    chunk = width // (2 * len(lead_refs))
    labels = lax.broadcasted_iota(jnp.int32, (width, width), 0)
    count = count_ref[0]

    def one(shift, place, out_ref):
        owner = lax.rem(ids_ref[0] + shift, row_size)
        def scan(k, state):
            chosen, seen = state
            hit = (lax.rem(rows_ref[k], row_size) == owner) & (k < count)
            chosen = jnp.where(hit & (seen == place), k, chosen)
            return chosen, seen + hit.astype(jnp.int32)

        chosen, seen = lax.fori_loop(0, slots, scan, (jnp.int32(0), jnp.int32(0)))
        row_hot = (labels == row_map_ref[pl.ds(chosen, 1), :]).astype(jnp.bfloat16)
        col_hot = (labels == col_map_ref[pl.ds(chosen, 1), :]).astype(jnp.bfloat16)
        left = tiles_ref[chosen]
        tile = None
        for _ in range(3):
            term = left.astype(jnp.bfloat16)
            left = left - term.astype(jnp.float32)
            moved = jnp.dot(row_hot, term, preferred_element_type=jnp.float32)
            moved = bf16_nt(moved.astype(jnp.bfloat16), col_hot)
            tile = moved if tile is None else tile + moved
        out_ref[place] = tile
        here = (seen > place) & (cols_ref[chosen] == 0)
        target = jnp.where(here, rows_ref[chosen] // row_size, -1).astype(jnp.float32)
        mark = jnp.full((8, width), target)
        for pair, lead_ref in enumerate(lead_refs):
            for side in range(2):
                first = (2 * pair + side) * chunk
                lead_ref[side, shift, pl.ds(place * chunk, chunk), :] = tile[first : first + chunk]
                lead_ref[side, shift, pl.ds(capacity * chunk + place * 8, 8), :] = mark

    for shift, out_ref in enumerate(out_refs):
        for place in range(capacity):
            one(shift, place, out_ref)


def move_tiles(row_size, col_size, capacity, ids, rows, cols, count, tiles, row_maps, col_maps):
    slots, width = tiles.shape[0], tiles.shape[1]
    smem = pl.BlockSpec(memory_space=pltpu.SMEM)
    vmem = pl.BlockSpec(memory_space=pltpu.VMEM)
    return pl.pallas_call(
        functools.partial(move_kernel, row_size, capacity),
        out_shape=[jax.ShapeDtypeStruct((capacity, width, width), jnp.float32)] * row_size
        + [
            jax.ShapeDtypeStruct(
                (2, row_size, capacity * (width // col_size + 8), width), jnp.float32
            )
        ]
        * (col_size // 2),
        in_specs=[smem, smem, smem, smem, vmem, vmem, vmem],
        out_specs=[vmem] * (row_size + col_size // 2),
        compiler_params=pltpu.CompilerParams(vmem_limit_bytes=VMEM_LIMIT),
        name="move_tiles",
    )(ids, rows, cols, count, tiles, row_maps, col_maps)


def locate_kernel(row_size, capacity, slots, ids_ref, meta_ref, own_ref):
    my_row = ids_ref[0]

    def clear(n, carry):
        own_ref[0, n] = -1
        own_ref[1, n] = -1
        return carry

    lax.fori_loop(0, row_size * capacity, clear, 0)

    def source(s, carry):
        line = lax.rem(my_row + row_size - s, row_size)
        count = meta_ref[line, 2 * slots]

        def slot(k, seen):
            target = meta_ref[line, k]
            hit = (lax.rem(target, row_size) == my_row) & (k < count)

            @pl.when(hit)
            def _():
                own_ref[0, s * capacity + seen] = target // row_size
                own_ref[1, s * capacity + seen] = meta_ref[line, slots + k]

            return jnp.minimum(seen + hit.astype(jnp.int32), capacity - 1)

        lax.fori_loop(0, slots, slot, jnp.int32(0))
        return carry

    lax.fori_loop(0, row_size, source, 0)


def locate(row_size, capacity, slots, ids, meta):
    smem = pl.BlockSpec(memory_space=pltpu.SMEM)
    return pl.pallas_call(
        functools.partial(locate_kernel, row_size, capacity, slots),
        out_shape=jax.ShapeDtypeStruct((2, row_size * capacity), jnp.int32),
        in_specs=[smem, smem],
        out_specs=smem,
        name="locate",
    )(ids, meta)


def first_kernel(front_ref, out_ref, buf, sem):
    row_tiles, chunk, col_size = front_ref.shape[0], front_ref.shape[2], front_ref.shape[4]
    copies = [
        pltpu.make_async_copy(
            front_ref.at[:, 0, :, 0, :, pl.ds(half * LANES, LANES)], buf.at[half], sem.at[half]
        )
        for half in range(2)
    ]
    for copy in copies:
        copy.start()
    for copy in copies:
        copy.wait()
    for half in range(2):
        flat = buf.at[half].reshape(row_tiles * chunk * col_size, LANES)
        for a in range(row_tiles):
            out_ref[a, :, half * LANES : (half + 1) * LANES] = flat[
                pl.ds(a * chunk * col_size, chunk, stride=col_size), :
            ]


def first_rows(front):
    row_tiles, chunk, col_size, width = front.shape[0], front.shape[2], front.shape[4], front.shape[5]
    return pl.pallas_call(
        first_kernel,
        out_shape=jax.ShapeDtypeStruct((row_tiles, chunk, width), jnp.float32),
        in_specs=[pl.BlockSpec(memory_space=pltpu.HBM)],
        out_specs=pl.BlockSpec(memory_space=pltpu.VMEM),
        scratch_shapes=[
            pltpu.VMEM((2, row_tiles, chunk, col_size, LANES), jnp.float32),
            pltpu.SemaphoreType.DMA((2,)),
        ],
        compiler_params=pltpu.CompilerParams(vmem_limit_bytes=VMEM_LIMIT),
        name="first_rows",
    )(front)


def lead_kernel(capacity, own_ref, *refs):
    kids_refs, out_ref = refs[:-1], refs[-1]
    chunk = own_ref.shape[1]

    def one(a, carry):
        total = own_ref[a]
        for kids_ref in kids_refs:
            for place in range(capacity):
                kid = kids_ref[pl.ds(place * chunk, chunk), :]
                target = kids_ref[pl.ds(capacity * chunk + place * 8, 1), :]
                total += jnp.where(target == a.astype(jnp.float32), kid, 0.0)
        out_ref[a] = total
        return carry

    lax.fori_loop(0, own_ref.shape[0], one, 0)


def lead_rows(capacity, own, kids):
    vmem = pl.BlockSpec(memory_space=pltpu.VMEM)
    return pl.pallas_call(
        functools.partial(lead_kernel, capacity),
        out_shape=jax.ShapeDtypeStruct(own.shape, jnp.float32),
        in_specs=[vmem] * (1 + len(kids)),
        out_specs=vmem,
        compiler_params=pltpu.CompilerParams(vmem_limit_bytes=VMEM_LIMIT),
        name="lead_rows",
    )(own, *kids)


def order_kernel(ids_ref, *refs):
    same, other_ref, out_ref = refs[:-2], refs[-2], refs[-1]
    for k, same_ref in enumerate(same):
        out_ref[lax.bitwise_xor(ids_ref[1], 2 * k)] = same_ref[...]
        out_ref[lax.bitwise_xor(ids_ref[1], 2 * k + 1)] = other_ref[k]


def order_rows(ids, same, other):
    smem = pl.BlockSpec(memory_space=pltpu.SMEM)
    vmem = pl.BlockSpec(memory_space=pltpu.VMEM)
    return pl.pallas_call(
        order_kernel,
        out_shape=jax.ShapeDtypeStruct((2 * len(same),) + same[0].shape, jnp.float32),
        in_specs=[smem] + [vmem] * (1 + len(same)),
        out_specs=vmem,
        compiler_params=pltpu.CompilerParams(vmem_limit_bytes=VMEM_LIMIT),
        name="order_rows",
    )(ids, *same, other)


def halves_of(value):
    high = value.astype(jnp.bfloat16)
    return high, (value - high.astype(jnp.float32)).astype(jnp.bfloat16)


def panel_kernel(ids_ref, inverse_ref, factor_ref, rows_ref, cols_ref, row_out, high_out, low_out):
    width = inverse_ref.shape[0]
    inverse = inverse_ref[...]

    def row(a, carry):
        row_out[a] = dot_nt(rows_ref[:, a].reshape(width, width), inverse)
        return carry

    lax.fori_loop(0, row_out.shape[0], row, 0)

    @pl.when(ids_ref[0] == 0)
    def _():
        row_out[0] = factor_ref[...]

    def column(b, carry):
        col = dot_nt(cols_ref[:, b].reshape(width, width), inverse)
        high_out[b], low_out[b] = halves_of(col)
        return carry

    lax.fori_loop(0, high_out.shape[0], column, 0)


def panels(ids, inverse, factor, rows, cols):
    smem = pl.BlockSpec(memory_space=pltpu.SMEM)
    vmem = pl.BlockSpec(memory_space=pltpu.VMEM)
    width = inverse.shape[0]
    return pl.pallas_call(
        panel_kernel,
        out_shape=(
            jax.ShapeDtypeStruct((rows.shape[1], width, width), jnp.float32),
            jax.ShapeDtypeStruct((cols.shape[1], width, width), jnp.bfloat16),
            jax.ShapeDtypeStruct((cols.shape[1], width, width), jnp.bfloat16),
        ),
        in_specs=[smem, vmem, vmem, vmem, vmem],
        out_specs=(vmem, vmem, vmem),
        compiler_params=pltpu.CompilerParams(vmem_limit_bytes=VMEM_LIMIT),
        name="panels",
    )(ids, inverse, factor, rows, cols)


def pack_kernel(depths, counts, front_ref, out_ref, in_buf, out_buf, in_sem, out_sem):
    col_size = front_ref.shape[4]
    chunk = front_ref.shape[2]

    def fetch(i):
        a, nb, slot = depths[i], counts[i], i % 2
        return [
            pltpu.make_async_copy(
                front_ref.at[a, 0, :, pl.ds(0, nb), :, pl.ds(half * LANES, LANES)],
                in_buf.at[slot, half, :, pl.ds(0, nb)],
                in_sem.at[slot, half],
            )
            for half in range(2)
        ]

    def send(i):
        first, nb, slot = sum(counts[:i]), counts[i], i % 2
        return pltpu.make_async_copy(
            out_buf.at[slot, :, pl.ds(0, nb)], out_ref.at[:, pl.ds(first, nb)], out_sem.at[slot]
        )

    steps = len(depths)
    for copy in fetch(0):
        copy.start()
    for i in range(steps):
        slot, nb = i % 2, counts[i]
        if i + 1 < steps:
            for copy in fetch(i + 1):
                copy.start()
        for copy in fetch(i):
            copy.wait()
        if i >= 2:
            send(i - 2).wait()
        for half in range(2):
            total = in_buf.shape[3]
            flat = in_buf.at[slot, half].reshape(chunk * total * col_size, LANES)
            for b in range(nb):
                for c in range(col_size):
                    out_buf[slot, c, b, :, half * LANES : (half + 1) * LANES] = flat[
                        pl.ds(b * col_size + c, chunk, stride=total * col_size), :
                    ]
        send(i).start()
    for i in range(max(steps - 2, 0), steps):
        send(i).wait()


def pack(front, depths, counts):
    chunk, col_size, width = front.shape[2], front.shape[4], front.shape[5]
    most = max(counts)
    return pl.pallas_call(
        functools.partial(pack_kernel, depths, counts),
        out_shape=jax.ShapeDtypeStruct((col_size, sum(counts), chunk, width), jnp.float32),
        in_specs=[pl.BlockSpec(memory_space=pltpu.HBM)],
        out_specs=pl.BlockSpec(memory_space=pltpu.HBM),
        scratch_shapes=[
            pltpu.VMEM((2, 2, chunk, most, col_size, LANES), jnp.float32),
            pltpu.VMEM((2, col_size, most, chunk, width), jnp.float32),
            pltpu.SemaphoreType.DMA((2, 2)),
            pltpu.SemaphoreType.DMA((2,)),
        ],
        compiler_params=pltpu.CompilerParams(vmem_limit_bytes=VMEM_LIMIT),
        name="pack",
    )(front)


def edge_kernel(blocks, ids_ref, front_ref, *refs):
    out_refs, (buf, sem) = refs[:-2], refs[-2:]
    chunk, col_size = front_ref.shape[2], front_ref.shape[4]
    copies = [
        pltpu.make_async_copy(
            front_ref.at[a, 0, :, b, :, pl.ds(half * LANES, LANES)], buf.at[i, half], sem.at[i, half]
        )
        for i, (a, b) in enumerate(blocks)
        for half in range(2)
    ]
    for copy in copies:
        copy.start()
    for copy in copies:
        copy.wait()
    for i in range(len(blocks)):
        for half in range(2):
            flat = buf.at[i, half].reshape(chunk * col_size, LANES)
            for k, out_ref in enumerate(out_refs):
                out_ref[i, :, half * LANES : (half + 1) * LANES] = flat[
                    pl.ds(lax.bitwise_xor(ids_ref[1], k), chunk, stride=col_size), :
                ]


def pack_edge(ids, front, blocks):
    chunk, col_size, width = front.shape[2], front.shape[4], front.shape[5]
    vmem = pl.BlockSpec(memory_space=pltpu.VMEM)
    return pl.pallas_call(
        functools.partial(edge_kernel, blocks),
        out_shape=[jax.ShapeDtypeStruct((len(blocks), chunk, width), jnp.float32)] * col_size,
        in_specs=[pl.BlockSpec(memory_space=pltpu.SMEM), pl.BlockSpec(memory_space=pltpu.HBM)],
        out_specs=[vmem] * col_size,
        scratch_shapes=[
            pltpu.VMEM((len(blocks), 2, chunk, col_size, LANES), jnp.float32),
            pltpu.SemaphoreType.DMA((len(blocks), 2)),
        ],
        compiler_params=pltpu.CompilerParams(vmem_limit_bytes=VMEM_LIMIT),
        name="pack_edge",
    )(ids, front)


def finish_kernel(
    depths,
    shared,
    edges,
    row_size,
    col_size,
    ids_ref,
    own_ref,
    recv_ref,
    rows_ref,
    high_ref,
    low_ref,
    kids_ref,
    *rest,
):
    edge_refs = rest[:col_size]
    out_ref, in_buf, row_buf, out_buf, high_buf, low_buf, kid_buf, *sems = rest[-13:]
    in_sem, row_sem, out_sem, col_sem, kid_sem, edge_sem = sems
    my_row, my_col = ids_ref[0], ids_ref[1]
    width = high_ref.shape[1]
    chunk = width // col_size
    halves = width // LANES
    blocks = high_ref.shape[0]
    stride = blocks * halves

    counts = [n + (edge is not None) for n, edge in zip(shared, edges)]

    def fetch(i):
        a, nb, edge, slot, first = depths[i], shared[i], edges[i], i % 2, sum(shared[:i])
        copies = [pltpu.make_async_copy(rows_ref.at[a], row_buf.at[slot], row_sem.at[slot])]
        if nb:
            copies.append(
                pltpu.make_async_copy(
                    recv_ref.at[:, pl.ds(first, nb)],
                    in_buf.at[slot, :, pl.ds(0, nb)],
                    in_sem.at[slot],
                )
            )
        if edge is not None:
            for k, edge_ref in enumerate(edge_refs):
                copies.append(
                    pltpu.make_async_copy(
                        edge_ref.at[edge],
                        in_buf.at[slot, lax.bitwise_xor(my_col, k), nb],
                        edge_sem.at[slot, k],
                    )
                )
        return copies

    def send(i):
        return pltpu.make_async_copy(out_buf.at[i % 2], out_ref.at[depths[i]], out_sem.at[i % 2])

    most = high_buf.shape[0]
    columns = [
        pltpu.make_async_copy(high_ref.at[pl.ds(0, most)], high_buf, col_sem.at[0]),
        pltpu.make_async_copy(low_ref.at[pl.ds(0, most)], low_buf, col_sem.at[1]),
    ]
    steps = len(depths)
    for copy in (*fetch(0), *columns):
        copy.start()
    for i in range(steps):
        a, nb, slot = depths[i], counts[i], i % 2
        if i + 1 < steps:
            for copy in fetch(i + 1):
                copy.start()
        for copy in fetch(i):
            copy.wait()
        if i == 0:
            for copy in columns:
                copy.wait()
        if i >= 2:
            send(i - 2).wait()
        for n in range(kids_ref.shape[0]):

            @pl.when(own_ref[0, n] == a)
            def _():
                copy = pltpu.make_async_copy(kids_ref.at[n], kid_buf, kid_sem)
                copy.start()
                copy.wait()
                in_buf[slot, :, own_ref[1, n]] += kid_buf[...].reshape(col_size, chunk, width)

        tile_i = a * row_size + my_row

        def store(b, tile):
            for half in range(halves):
                out_buf[slot, pl.ds(b * halves + half, width, stride=stride), :] = tile[
                    :, half * LANES : (half + 1) * LANES
                ]

        row_high, row_low = halves_of(row_buf[slot])

        def update(b):
            return bf16_nt(row_high, high_buf[b]) + (
                bf16_nt(row_high, low_buf[b]) + bf16_nt(row_low, high_buf[b])
            )

        for b in range(nb):
            tile = in_buf[slot, :, b].reshape(width, width)
            tile_j = b * col_size + my_col
            if b < nb - 1:
                store(b, tile - update(b))
            else:

                @pl.when(tile_i > tile_j)
                def _():
                    store(b, tile - update(b))

                @pl.when(tile_i == tile_j)
                def _():
                    store(b, 0.5 * (tile + tile.T) - update(b))

                @pl.when(tile_i < tile_j)
                def _():
                    store(b, jnp.zeros_like(tile))

        @pl.when(my_col == 0)
        def _():
            store(0, row_buf[slot])

        zero = jnp.zeros((width, LANES), jnp.float32)
        for n in range(nb * halves, stride):
            out_buf[slot, pl.ds(n, width, stride=stride), :] = zero
        send(i).start()
    for i in range(max(steps - 2, 0), steps):
        send(i).wait()


def finish(
    depths, shared, edges, row_size, col_size, ids, own, recv, rows, high, low, kids, edge, out=None
):
    smem = pl.BlockSpec(memory_space=pltpu.SMEM)
    hbm = pl.BlockSpec(memory_space=pltpu.HBM)
    blocks, width = high.shape[0], high.shape[1]
    chunk = width // col_size
    lines = width * blocks * (width // LANES)
    counts = [n + (edge is not None) for n, edge in zip(shared, edges)]
    operands = [ids, own, recv, rows, high, low, kids, *edge]
    in_specs = [smem, smem] + [hbm] * (5 + len(edge))
    aliases = {}
    if out is not None:
        operands.append(out)
        in_specs.append(hbm)
        aliases = {len(operands) - 1: 0}
    return pl.pallas_call(
        functools.partial(finish_kernel, depths, shared, edges, row_size, col_size),
        out_shape=jax.ShapeDtypeStruct((rows.shape[0], lines, LANES), jnp.float32),
        in_specs=in_specs,
        out_specs=hbm,
        scratch_shapes=[
            pltpu.VMEM((2, col_size, max(counts), chunk, width), jnp.float32),
            pltpu.VMEM((2, width, width), jnp.float32),
            pltpu.VMEM((2, lines, LANES), jnp.float32),
            pltpu.VMEM((max(counts), width, width), jnp.bfloat16),
            pltpu.VMEM((max(counts), width, width), jnp.bfloat16),
            pltpu.VMEM((width, width), jnp.float32),
            pltpu.SemaphoreType.DMA((2,)),
            pltpu.SemaphoreType.DMA((2,)),
            pltpu.SemaphoreType.DMA((2,)),
            pltpu.SemaphoreType.DMA((2,)),
            pltpu.SemaphoreType.DMA,
            pltpu.SemaphoreType.DMA((2, col_size)),
        ],
        input_output_aliases=aliases,
        compiler_params=pltpu.CompilerParams(vmem_limit_bytes=VMEM_LIMIT),
        name="finish",
    )(*operands)


def on_device(front, child_tiles, child_rows, child_cols, child_counts, row_maps, col_maps):
    row_size, col_size = lax.axis_size("row"), lax.axis_size("col")
    my_row, my_col = lax.axis_index("row"), lax.axis_index("col")
    row_tiles, chunk, col_tiles, width = front.shape[0], front.shape[2], front.shape[3], front.shape[5]
    slots = child_tiles.shape[2]
    capacity = slots // 4
    arrivals = row_size * capacity
    group = col_size // row_size
    ids = jnp.stack([my_row, my_col]).astype(jnp.int32)

    shared = [shared_blocks(a, row_size, col_size) for a in range(row_tiles)]
    edge_blocks = [
        (a, shared[a]) for a in range(row_tiles) if depth_blocks(a, row_size, col_size) > shared[a]
    ]
    edge_of = {a: i for i, (a, _) in enumerate(edge_blocks)}
    last = (row_tiles - 5) * 3 // 4 + 1
    parts = [[row_tiles - 2], [row_tiles - 1, row_tiles - 3, row_tiles - 4]]
    parts.append([a for a in range(row_tiles - 5, -1, -1) if a != last])
    parts.append([last])

    def packed(part, *after):
        held = lax.optimization_barrier((front,) + after)[0]
        sent = [a for a in part if shared[a]]
        return pack(held, sent, [shared[a] for a in sent])

    def exchange(blocks, *after):
        blocks = lax.optimization_barrier((blocks,) + after)[0]
        return lax.all_to_all(blocks, "col", split_axis=0, concat_axis=0, tiled=True)

    def along_row(shift):
        return [(r, (r + shift) % row_size) for r in range(row_size)]

    def across_col(k):
        return [(c, c ^ k) for c in range(col_size)]

    moved = move_tiles(
        row_size,
        col_size,
        capacity,
        ids,
        child_rows.reshape(slots),
        child_cols.reshape(slots),
        child_counts.reshape(1),
        child_tiles.reshape(slots, width, width),
        row_maps.reshape(slots, width),
        col_maps.reshape(slots, width),
    )
    moved, pieces = moved[:row_size], moved[row_size:]

    sent = [
        lax.ppermute(pieces[pair], "col", [(0, 2 * pair)]) for pair in range(1, col_size // 2)
    ]
    edge = pack_edge(ids, lax.optimization_barrier((front, pieces[0]))[0], edge_blocks)

    def send_edge(k, value):
        steps = [
            (r * col_size + c, r * col_size + (c ^ k))
            for r in range(row_size)
            for c in range(col_size)
            if c ^ k <= r
        ]
        return lax.ppermute(value, ("row", "col"), steps)

    half = col_size // 2
    far = [send_edge(k, edge[k]) for k in range(half, col_size)]
    second = packed(parts[1], pieces[0])
    blocks = packed(parts[0], pieces[0])
    first = first_rows(front)
    meta = jnp.concatenate(
        [child_rows.reshape(1, slots), child_cols.reshape(1, slots), child_counts.reshape(1, 1)], axis=1
    )
    meta, _ = lax.optimization_barrier((meta, pieces[0]))
    meta = lax.all_gather(meta, "row", axis=0, tiled=True)
    own = locate(row_size, capacity, slots, ids, meta)
    *sent, second, first, own = lax.optimization_barrier((*sent, second, first, own))
    arrived = [exchange(blocks, *sent, *far)]
    lead = jnp.where(my_col == 0, pieces[0], sum(sent[1:], sent[0]))
    other = lax.ppermute(lead[1], "col", [(c, c + 1) for c in range(0, col_size, 2)])
    lead = jnp.where(my_col % 2 == 0, lead[0], other)
    lead = [lead[0]] + [
        lax.ppermute(lead[shift], "row", along_row(shift)) for shift in range(1, row_size)
    ]
    raw = lead_rows(capacity, first, lead)

    same = [raw] + [lax.ppermute(raw, "col", across_col(k)) for k in range(2, col_size, 2)]
    near = [send_edge(k, lax.optimization_barrier((edge[k], raw))[0]) for k in range(1, half)]
    arrived.append(exchange(second, arrived[0], *same, *near))
    other = lax.ppermute(jnp.stack(same), "col", across_col(1))
    raw_rows = order_rows(ids, same, other)
    arrived.append(exchange(packed(parts[2], same[1]), arrived[1], other))
    edge = [edge[0], *near, *far]

    *moved, _ = lax.optimization_barrier((*moved, raw))
    kids = jnp.concatenate(
        [moved[0]]
        + [lax.ppermute(moved[shift], "row", along_row(shift)) for shift in range(1, row_size)]
    )

    corner_mine = corner = raw_rows[:, 0].reshape(width, width)
    corner = jnp.where(my_row == 0, corner, 0.0)
    for shift in range(1, row_size):
        corner = corner + lax.ppermute(corner_mine, "row", [(0, shift)])
    corner = 0.5 * (corner + corner.T)
    factor = jnp.linalg.cholesky(corner)
    inverse = jax.scipy.linalg.solve_triangular(
        factor, jnp.eye(width, dtype=jnp.float32), lower=True
    )

    mine = lax.dynamic_index_in_dim(
        raw_rows.reshape(col_size, col_tiles, group, chunk, width),
        my_col // row_size,
        2,
        keepdims=False,
    )
    raw_cols = jnp.where(my_row == my_col % row_size, mine, 0.0)
    for shift in range(1, row_size):
        steps = [
            ((c % row_size) * col_size + c, ((c + shift) % row_size) * col_size + c)
            for c in range(col_size)
        ]
        raw_cols = raw_cols + lax.ppermute(mine, ("row", "col"), steps)
    rows, high, low = panels(ids, inverse, factor, raw_rows, raw_cols)

    out = None
    for step, part in enumerate(parts):
        if step == 2:
            arrived.append(exchange(packed(parts[3]), arrived[2], out))
        out = finish(
            part,
            [shared[a] for a in part],
            [edge_of.get(a) for a in part],
            row_size,
            col_size,
            ids,
            own,
            arrived[step],
            rows,
            high,
            low,
            kids,
            edge,
            out,
        )
    return out.reshape(row_tiles, 1, width, col_tiles, 1, width)


def solution(mesh):
    return jax.shard_map(
        on_device,
        mesh=mesh,
        in_specs=(
            P(None, "row", "col", None, None, None),
            P("row", "col", None, None, None),
            P("row", "col", None),
            P("row", "col", None),
            P("row", "col"),
            P("row", "col", None, None),
            P("row", "col", None, None),
        ),
        out_specs=P(None, "row", None, None, "col", None),
        check_vma=False,
    )
```

```python
import functools

import jax
import jax.numpy as jnp
from jax import lax
from jax.experimental import pallas as pl
from jax.experimental.pallas import tpu as pltpu
from jax.sharding import PartitionSpec as P

HIGHEST = lax.Precision.HIGHEST
LANES = 128
VMEM_LIMIT = 60 << 20


def bf16_nt(left, right):
    return lax.dot_general(
        left, right, (((1,), (1,)), ((), ())), preferred_element_type=jnp.float32
    )


def depth_blocks(a, row_size, col_size):
    return (a * row_size + row_size - 1) // col_size + 1


def shared_blocks(a, row_size, col_size):
    return (a * row_size + row_size - 1 - col_size // 2) // col_size + 1


def move_kernel(
    row_size,
    capacity,
    ids_ref,
    rows_ref,
    cols_ref,
    count_ref,
    tiles_ref,
    row_map_ref,
    col_map_ref,
    *out_refs,
):
    slots, width = tiles_ref.shape[0], tiles_ref.shape[1]
    out_refs, lead_refs = out_refs[:row_size], out_refs[row_size:]
    chunk = width // (2 * len(lead_refs))
    labels = lax.broadcasted_iota(jnp.int32, (width, width), 0)
    count = count_ref[0]

    def one(shift, place, out_ref):
        owner = lax.rem(ids_ref[0] + shift, row_size)
        def scan(k, state):
            chosen, seen = state
            hit = (lax.rem(rows_ref[k], row_size) == owner) & (k < count)
            chosen = jnp.where(hit & (seen == place), k, chosen)
            return chosen, seen + hit.astype(jnp.int32)

        chosen, seen = lax.fori_loop(0, slots, scan, (jnp.int32(0), jnp.int32(0)))
        row_hot = (labels == row_map_ref[pl.ds(chosen, 1), :]).astype(jnp.bfloat16)
        col_hot = (labels == col_map_ref[pl.ds(chosen, 1), :]).astype(jnp.bfloat16)
        left = tiles_ref[chosen]
        tile = None
        for _ in range(3):
            term = left.astype(jnp.bfloat16)
            left = left - term.astype(jnp.float32)
            moved = jnp.dot(row_hot, term, preferred_element_type=jnp.float32)
            moved = bf16_nt(moved.astype(jnp.bfloat16), col_hot)
            tile = moved if tile is None else tile + moved
        out_ref[place] = tile
        here = (seen > place) & (cols_ref[chosen] == 0)
        target = jnp.where(here, rows_ref[chosen] // row_size, -1).astype(jnp.float32)
        mark = jnp.full((1, width), target)
        for pair, lead_ref in enumerate(lead_refs):
            for side in range(2):
                first = (2 * pair + side) * chunk
                lead_ref[side, shift, pl.ds(place * chunk, chunk), :] = tile[first : first + chunk]
                lead_ref[side, shift, pl.ds(capacity * chunk + place, 1), :] = mark

    for shift, out_ref in enumerate(out_refs):
        for place in range(capacity):
            one(shift, place, out_ref)


def move_tiles(row_size, col_size, capacity, ids, rows, cols, count, tiles, row_maps, col_maps):
    slots, width = tiles.shape[0], tiles.shape[1]
    smem = pl.BlockSpec(memory_space=pltpu.SMEM)
    vmem = pl.BlockSpec(memory_space=pltpu.VMEM)
    return pl.pallas_call(
        functools.partial(move_kernel, row_size, capacity),
        out_shape=[jax.ShapeDtypeStruct((capacity, width, width), jnp.float32)] * row_size
        + [
            jax.ShapeDtypeStruct(
                (2, row_size, capacity * (width // col_size) + 8, width), jnp.float32
            )
        ]
        * (col_size // 2),
        in_specs=[smem, smem, smem, smem, vmem, vmem, vmem],
        out_specs=[vmem] * (row_size + col_size // 2),
        compiler_params=pltpu.CompilerParams(vmem_limit_bytes=VMEM_LIMIT),
        name="move_tiles",
    )(ids, rows, cols, count, tiles, row_maps, col_maps)


def locate_kernel(row_size, capacity, slots, ids_ref, meta_ref, own_ref):
    my_row = ids_ref[0]

    def clear(n, carry):
        own_ref[0, n] = -1
        own_ref[1, n] = -1
        return carry

    lax.fori_loop(0, row_size * capacity, clear, 0)

    def source(s, carry):
        line = lax.rem(my_row + row_size - s, row_size)
        count = meta_ref[line, 2 * slots]

        def slot(k, seen):
            target = meta_ref[line, k]
            hit = (lax.rem(target, row_size) == my_row) & (k < count)

            @pl.when(hit)
            def _():
                own_ref[0, s * capacity + seen] = target // row_size
                own_ref[1, s * capacity + seen] = meta_ref[line, slots + k]

            return jnp.minimum(seen + hit.astype(jnp.int32), capacity - 1)

        lax.fori_loop(0, slots, slot, jnp.int32(0))
        return carry

    lax.fori_loop(0, row_size, source, 0)


def locate(row_size, capacity, slots, ids, meta):
    smem = pl.BlockSpec(memory_space=pltpu.SMEM)
    return pl.pallas_call(
        functools.partial(locate_kernel, row_size, capacity, slots),
        out_shape=jax.ShapeDtypeStruct((2, row_size * capacity), jnp.int32),
        in_specs=[smem, smem],
        out_specs=smem,
        name="locate",
    )(ids, meta)


def first_kernel(front_ref, out_ref, buf, sem):
    row_tiles, chunk, col_size = front_ref.shape[0], front_ref.shape[2], front_ref.shape[4]
    copies = [
        pltpu.make_async_copy(
            front_ref.at[:, 0, :, 0, :, pl.ds(half * LANES, LANES)], buf.at[half], sem.at[half]
        )
        for half in range(2)
    ]
    for copy in copies:
        copy.start()
    for copy in copies:
        copy.wait()
    for half in range(2):
        flat = buf.at[half].reshape(row_tiles * chunk * col_size, LANES)
        for a in range(row_tiles):
            out_ref[a, :, half * LANES : (half + 1) * LANES] = flat[
                pl.ds(a * chunk * col_size, chunk, stride=col_size), :
            ]


def first_rows(front):
    row_tiles, chunk, col_size, width = front.shape[0], front.shape[2], front.shape[4], front.shape[5]
    return pl.pallas_call(
        first_kernel,
        out_shape=jax.ShapeDtypeStruct((row_tiles, chunk, width), jnp.float32),
        in_specs=[pl.BlockSpec(memory_space=pltpu.HBM)],
        out_specs=pl.BlockSpec(memory_space=pltpu.VMEM),
        scratch_shapes=[
            pltpu.VMEM((2, row_tiles, chunk, col_size, LANES), jnp.float32),
            pltpu.SemaphoreType.DMA((2,)),
        ],
        compiler_params=pltpu.CompilerParams(vmem_limit_bytes=VMEM_LIMIT),
        name="first_rows",
    )(front)


def lead_kernel(capacity, own_ref, *refs):
    kids_refs, out_ref = refs[:-1], refs[-1]
    chunk = own_ref.shape[1]

    def one(a, carry):
        total = own_ref[a]
        for kids_ref in kids_refs:
            for place in range(capacity):
                kid = kids_ref[pl.ds(place * chunk, chunk), :]
                target = kids_ref[pl.ds(capacity * chunk + place, 1), :]
                total += jnp.where(target == a.astype(jnp.float32), kid, 0.0)
        out_ref[a] = total
        return carry

    lax.fori_loop(0, own_ref.shape[0], one, 0)


def lead_rows(capacity, own, kids):
    vmem = pl.BlockSpec(memory_space=pltpu.VMEM)
    return pl.pallas_call(
        functools.partial(lead_kernel, capacity),
        out_shape=jax.ShapeDtypeStruct(own.shape, jnp.float32),
        in_specs=[vmem] * (1 + len(kids)),
        out_specs=vmem,
        compiler_params=pltpu.CompilerParams(vmem_limit_bytes=VMEM_LIMIT),
        name="lead_rows",
    )(own, *kids)


def order_kernel(ids_ref, *refs):
    same, other_ref, out_ref = refs[:-2], refs[-2], refs[-1]
    for k, same_ref in enumerate(same):
        out_ref[lax.bitwise_xor(ids_ref[1], 2 * k)] = same_ref[...]
        out_ref[lax.bitwise_xor(ids_ref[1], 2 * k + 1)] = other_ref[k]


def order_rows(ids, same, other):
    smem = pl.BlockSpec(memory_space=pltpu.SMEM)
    vmem = pl.BlockSpec(memory_space=pltpu.VMEM)
    return pl.pallas_call(
        order_kernel,
        out_shape=jax.ShapeDtypeStruct((2 * len(same),) + same[0].shape, jnp.float32),
        in_specs=[smem] + [vmem] * (1 + len(same)),
        out_specs=vmem,
        compiler_params=pltpu.CompilerParams(vmem_limit_bytes=VMEM_LIMIT),
        name="order_rows",
    )(ids, *same, other)


def halves_of(value):
    high = value.astype(jnp.bfloat16)
    return high, (value - high.astype(jnp.float32)).astype(jnp.bfloat16)


def panel_kernel(ids_ref, inverse_ref, factor_ref, rows_ref, cols_ref, row_out, high_out, low_out):
    width = inverse_ref.shape[0]
    high, low = halves_of(inverse_ref[...])

    def solve(tile):
        tile_high, tile_low = halves_of(tile)
        return bf16_nt(tile_high, high) + (bf16_nt(tile_high, low) + bf16_nt(tile_low, high))

    def row(a, carry):
        row_out[a] = solve(rows_ref[:, a].reshape(width, width))
        return carry

    lax.fori_loop(0, row_out.shape[0], row, 0)

    @pl.when(ids_ref[0] == 0)
    def _():
        row_out[0] = factor_ref[...]

    def column(b, carry):
        col = solve(cols_ref[:, b].reshape(width, width))
        high_out[b], low_out[b] = halves_of(col)
        return carry

    lax.fori_loop(0, high_out.shape[0], column, 0)


def panels(ids, inverse, factor, rows, cols):
    smem = pl.BlockSpec(memory_space=pltpu.SMEM)
    vmem = pl.BlockSpec(memory_space=pltpu.VMEM)
    width = inverse.shape[0]
    return pl.pallas_call(
        panel_kernel,
        out_shape=(
            jax.ShapeDtypeStruct((rows.shape[1], width, width), jnp.float32),
            jax.ShapeDtypeStruct((cols.shape[1], width, width), jnp.bfloat16),
            jax.ShapeDtypeStruct((cols.shape[1], width, width), jnp.bfloat16),
        ),
        in_specs=[smem, vmem, vmem, vmem, vmem],
        out_specs=(vmem, vmem, vmem),
        compiler_params=pltpu.CompilerParams(vmem_limit_bytes=VMEM_LIMIT),
        name="panels",
    )(ids, inverse, factor, rows, cols)


def pack_kernel(depths, counts, front_ref, out_ref, in_buf, out_buf, in_sem, out_sem):
    col_size = front_ref.shape[4]
    chunk = front_ref.shape[2]

    def fetch(i):
        a, nb, slot = depths[i], counts[i], i % 2
        return [
            pltpu.make_async_copy(
                front_ref.at[a, 0, :, pl.ds(0, nb), :, pl.ds(half * LANES, LANES)],
                in_buf.at[slot, half, :, pl.ds(0, nb)],
                in_sem.at[slot, half],
            )
            for half in range(2)
        ]

    def send(i):
        first, nb, slot = sum(counts[:i]), counts[i], i % 2
        return pltpu.make_async_copy(
            out_buf.at[slot, :, pl.ds(0, nb)], out_ref.at[:, pl.ds(first, nb)], out_sem.at[slot]
        )

    steps = len(depths)
    for copy in fetch(0):
        copy.start()
    for i in range(steps):
        slot, nb = i % 2, counts[i]
        if i + 1 < steps:
            for copy in fetch(i + 1):
                copy.start()
        for copy in fetch(i):
            copy.wait()
        if i >= 2:
            send(i - 2).wait()
        for half in range(2):
            total = in_buf.shape[3]
            flat = in_buf.at[slot, half].reshape(chunk * total * col_size, LANES)
            for b in range(nb):
                for c in range(col_size):
                    out_buf[slot, c, b, :, half * LANES : (half + 1) * LANES] = flat[
                        pl.ds(b * col_size + c, chunk, stride=total * col_size), :
                    ]
        send(i).start()
    for i in range(max(steps - 2, 0), steps):
        send(i).wait()


def pack(front, depths, counts):
    chunk, col_size, width = front.shape[2], front.shape[4], front.shape[5]
    most = max(counts)
    return pl.pallas_call(
        functools.partial(pack_kernel, depths, counts),
        out_shape=jax.ShapeDtypeStruct((col_size, sum(counts), chunk, width), jnp.float32),
        in_specs=[pl.BlockSpec(memory_space=pltpu.HBM)],
        out_specs=pl.BlockSpec(memory_space=pltpu.HBM),
        scratch_shapes=[
            pltpu.VMEM((2, 2, chunk, most, col_size, LANES), jnp.float32),
            pltpu.VMEM((2, col_size, most, chunk, width), jnp.float32),
            pltpu.SemaphoreType.DMA((2, 2)),
            pltpu.SemaphoreType.DMA((2,)),
        ],
        compiler_params=pltpu.CompilerParams(vmem_limit_bytes=VMEM_LIMIT),
        name="pack",
    )(front)


def edge_kernel(blocks, ids_ref, front_ref, *refs):
    out_refs, (buf, sem) = refs[:-2], refs[-2:]
    chunk, col_size = front_ref.shape[2], front_ref.shape[4]
    copies = [
        pltpu.make_async_copy(
            front_ref.at[a, 0, :, b, :, pl.ds(half * LANES, LANES)], buf.at[i, half], sem.at[i, half]
        )
        for i, (a, b) in enumerate(blocks)
        for half in range(2)
    ]
    for copy in copies:
        copy.start()
    for copy in copies:
        copy.wait()
    for i in range(len(blocks)):
        for half in range(2):
            flat = buf.at[i, half].reshape(chunk * col_size, LANES)
            for k, out_ref in enumerate(out_refs):
                out_ref[i, :, half * LANES : (half + 1) * LANES] = flat[
                    pl.ds(lax.bitwise_xor(ids_ref[1], k), chunk, stride=col_size), :
                ]


def pack_edge(ids, front, blocks):
    chunk, col_size, width = front.shape[2], front.shape[4], front.shape[5]
    vmem = pl.BlockSpec(memory_space=pltpu.VMEM)
    return pl.pallas_call(
        functools.partial(edge_kernel, blocks),
        out_shape=[jax.ShapeDtypeStruct((len(blocks), chunk, width), jnp.float32)] * col_size,
        in_specs=[pl.BlockSpec(memory_space=pltpu.SMEM), pl.BlockSpec(memory_space=pltpu.HBM)],
        out_specs=[vmem] * col_size,
        scratch_shapes=[
            pltpu.VMEM((len(blocks), 2, chunk, col_size, LANES), jnp.float32),
            pltpu.SemaphoreType.DMA((len(blocks), 2)),
        ],
        compiler_params=pltpu.CompilerParams(vmem_limit_bytes=VMEM_LIMIT),
        name="pack_edge",
    )(ids, front)


def finish_kernel(
    depths,
    shared,
    edges,
    row_size,
    col_size,
    ids_ref,
    own_ref,
    recv_ref,
    rows_ref,
    high_ref,
    low_ref,
    kids_ref,
    *rest,
):
    edge_refs = rest[:col_size]
    out_ref, in_buf, row_buf, out_buf, high_buf, low_buf, kid_buf, *sems = rest[-13:]
    in_sem, row_sem, out_sem, col_sem, kid_sem, edge_sem = sems
    my_row, my_col = ids_ref[0], ids_ref[1]
    width = high_ref.shape[1]
    chunk = width // col_size
    halves = width // LANES
    blocks = high_ref.shape[0]
    stride = blocks * halves

    counts = [n + (edge is not None) for n, edge in zip(shared, edges)]

    def fetch(i):
        a, nb, edge, slot, first = depths[i], shared[i], edges[i], i % 2, sum(shared[:i])
        copies = [pltpu.make_async_copy(rows_ref.at[a], row_buf.at[slot], row_sem.at[slot])]
        if nb:
            copies.append(
                pltpu.make_async_copy(
                    recv_ref.at[:, pl.ds(first, nb)],
                    in_buf.at[slot, :, pl.ds(0, nb)],
                    in_sem.at[slot],
                )
            )
        if edge is not None:
            for k, edge_ref in enumerate(edge_refs):
                copies.append(
                    pltpu.make_async_copy(
                        edge_ref.at[edge],
                        in_buf.at[slot, lax.bitwise_xor(my_col, k), nb],
                        edge_sem.at[slot, k],
                    )
                )
        return copies

    def send(i):
        return pltpu.make_async_copy(out_buf.at[i % 2], out_ref.at[depths[i]], out_sem.at[i % 2])

    most = high_buf.shape[0]
    columns = [
        pltpu.make_async_copy(high_ref.at[pl.ds(0, most)], high_buf, col_sem.at[0]),
        pltpu.make_async_copy(low_ref.at[pl.ds(0, most)], low_buf, col_sem.at[1]),
    ]
    steps = len(depths)
    for copy in (*fetch(0), *columns):
        copy.start()
    for i in range(steps):
        a, nb, slot = depths[i], counts[i], i % 2
        if i + 1 < steps:
            for copy in fetch(i + 1):
                copy.start()
        for copy in fetch(i):
            copy.wait()
        if i == 0:
            for copy in columns:
                copy.wait()
        if i >= 2:
            send(i - 2).wait()
        for n in range(kids_ref.shape[0]):

            @pl.when(own_ref[0, n] == a)
            def _():
                copy = pltpu.make_async_copy(kids_ref.at[n], kid_buf, kid_sem)
                copy.start()
                copy.wait()
                in_buf[slot, :, own_ref[1, n]] += kid_buf[...].reshape(col_size, chunk, width)

        tile_i = a * row_size + my_row

        def store(b, tile):
            for half in range(halves):
                out_buf[slot, pl.ds(b * halves + half, width, stride=stride), :] = tile[
                    :, half * LANES : (half + 1) * LANES
                ]

        row_high, row_low = halves_of(row_buf[slot])

        def update(b):
            return bf16_nt(row_high, high_buf[b]) + (
                bf16_nt(row_high, low_buf[b]) + bf16_nt(row_low, high_buf[b])
            )

        for b in range(nb):
            tile = in_buf[slot, :, b].reshape(width, width)
            tile_j = b * col_size + my_col
            if b < nb - 1:
                store(b, tile - update(b))
            else:

                @pl.when(tile_i > tile_j)
                def _():
                    store(b, tile - update(b))

                @pl.when(tile_i == tile_j)
                def _():
                    store(b, 0.5 * (tile + tile.T) - update(b))

                @pl.when(tile_i < tile_j)
                def _():
                    store(b, jnp.zeros_like(tile))

        @pl.when(my_col == 0)
        def _():
            store(0, row_buf[slot])

        zero = jnp.zeros((width, LANES), jnp.float32)
        for n in range(nb * halves, stride):
            out_buf[slot, pl.ds(n, width, stride=stride), :] = zero
        send(i).start()
    for i in range(max(steps - 2, 0), steps):
        send(i).wait()


def finish(
    depths, shared, edges, row_size, col_size, ids, own, recv, rows, high, low, kids, edge, out=None
):
    smem = pl.BlockSpec(memory_space=pltpu.SMEM)
    hbm = pl.BlockSpec(memory_space=pltpu.HBM)
    blocks, width = high.shape[0], high.shape[1]
    chunk = width // col_size
    lines = width * blocks * (width // LANES)
    counts = [n + (edge is not None) for n, edge in zip(shared, edges)]
    operands = [ids, own, recv, rows, high, low, kids, *edge]
    in_specs = [smem, smem] + [hbm] * (5 + len(edge))
    aliases = {}
    if out is not None:
        operands.append(out)
        in_specs.append(hbm)
        aliases = {len(operands) - 1: 0}
    return pl.pallas_call(
        functools.partial(finish_kernel, depths, shared, edges, row_size, col_size),
        out_shape=jax.ShapeDtypeStruct((rows.shape[0], lines, LANES), jnp.float32),
        in_specs=in_specs,
        out_specs=hbm,
        scratch_shapes=[
            pltpu.VMEM((2, col_size, max(counts), chunk, width), jnp.float32),
            pltpu.VMEM((2, width, width), jnp.float32),
            pltpu.VMEM((2, lines, LANES), jnp.float32),
            pltpu.VMEM((max(counts), width, width), jnp.bfloat16),
            pltpu.VMEM((max(counts), width, width), jnp.bfloat16),
            pltpu.VMEM((width, width), jnp.float32),
            pltpu.SemaphoreType.DMA((2,)),
            pltpu.SemaphoreType.DMA((2,)),
            pltpu.SemaphoreType.DMA((2,)),
            pltpu.SemaphoreType.DMA((2,)),
            pltpu.SemaphoreType.DMA,
            pltpu.SemaphoreType.DMA((2, col_size)),
        ],
        input_output_aliases=aliases,
        compiler_params=pltpu.CompilerParams(vmem_limit_bytes=VMEM_LIMIT),
        name="finish",
    )(*operands)


def factor_and_inverse(corner):
    size = corner.shape[0] // 2
    eye = jnp.eye(size, dtype=jnp.float32)

    def both(block):
        factor = lax.linalg.cholesky(block, symmetrize_input=False)
        return factor, jax.scipy.linalg.solve_triangular(factor, eye, lower=True)

    def product(left, right):
        return jnp.dot(left, right, precision=HIGHEST)

    top, top_inverse = both(corner[:size, :size])
    below = product(corner[size:, :size], top_inverse.T)
    end, end_inverse = both(corner[size:, size:] - product(below, below.T))
    corner_inverse = -product(end_inverse, product(below, top_inverse))
    zero = jnp.zeros_like(eye)
    return (
        jnp.block([[top, zero], [below, end]]),
        jnp.block([[top_inverse, zero], [corner_inverse, end_inverse]]),
    )


def on_device(front, child_tiles, child_rows, child_cols, child_counts, row_maps, col_maps):
    row_size, col_size = lax.axis_size("row"), lax.axis_size("col")
    my_row, my_col = lax.axis_index("row"), lax.axis_index("col")
    row_tiles, chunk, col_tiles, width = front.shape[0], front.shape[2], front.shape[3], front.shape[5]
    slots = child_tiles.shape[2]
    capacity = slots // 4
    arrivals = row_size * capacity
    group = col_size // row_size
    ids = jnp.stack([my_row, my_col]).astype(jnp.int32)

    shared = [shared_blocks(a, row_size, col_size) for a in range(row_tiles)]
    edge_blocks = [
        (a, shared[a]) for a in range(row_tiles) if depth_blocks(a, row_size, col_size) > shared[a]
    ]
    edge_of = {a: i for i, (a, _) in enumerate(edge_blocks)}
    last = (row_tiles - 5) * 3 // 4 + 1
    parts = [[row_tiles - 2], [row_tiles - 1, row_tiles - 3, row_tiles - 4]]
    parts.append([a for a in range(row_tiles - 5, -1, -1) if a != last])
    parts.append([last])

    def packed(part, *after):
        held = lax.optimization_barrier((front,) + after)[0]
        sent = [a for a in part if shared[a]]
        return pack(held, sent, [shared[a] for a in sent])

    def exchange(blocks, *after):
        blocks = lax.optimization_barrier((blocks,) + after)[0]
        return lax.all_to_all(blocks, "col", split_axis=0, concat_axis=0, tiled=True)

    def along_row(shift):
        return [(r, (r + shift) % row_size) for r in range(row_size)]

    def across_col(k):
        return [(c, c ^ k) for c in range(col_size)]

    moved = move_tiles(
        row_size,
        col_size,
        capacity,
        ids,
        child_rows.reshape(slots),
        child_cols.reshape(slots),
        child_counts.reshape(1),
        child_tiles.reshape(slots, width, width),
        row_maps.reshape(slots, width),
        col_maps.reshape(slots, width),
    )
    moved, pieces = moved[:row_size], moved[row_size:]

    sent = [
        lax.ppermute(pieces[pair], "col", [(0, 2 * pair)]) for pair in range(1, col_size // 2)
    ]
    edge = pack_edge(ids, lax.optimization_barrier((front, pieces[0]))[0], edge_blocks)

    def send_edge(k, value):
        steps = [
            (r * col_size + c, r * col_size + (c ^ k))
            for r in range(row_size)
            for c in range(col_size)
            if c ^ k <= r
        ]
        return lax.ppermute(value, ("row", "col"), steps)

    half = col_size // 2
    far = [send_edge(k, edge[k]) for k in range(half, col_size)]
    second = packed(parts[1], pieces[0])
    blocks = packed(parts[0], pieces[0])
    first = first_rows(front)
    meta = jnp.concatenate(
        [child_rows.reshape(1, slots), child_cols.reshape(1, slots), child_counts.reshape(1, 1)], axis=1
    )
    meta, _ = lax.optimization_barrier((meta, pieces[0]))
    meta = lax.all_gather(meta, "row", axis=0, tiled=True)
    own = locate(row_size, capacity, slots, ids, meta)
    *sent, blocks, _ = lax.optimization_barrier((*sent, blocks, *far[:1]))
    arrived = [exchange(blocks, *sent, *far)]
    lead = jnp.where(my_col == 0, pieces[0], sum(sent[1:], sent[0]))
    other = lax.ppermute(lead[1], "col", [(c, c + 1) for c in range(0, col_size, 2)])
    other, second, first, own = lax.optimization_barrier((other, second, first, own))
    lead = jnp.where(my_col % 2 == 0, lead[0], other)
    lead = [lead[0]] + [
        lax.ppermute(lead[shift], "row", along_row(shift)) for shift in range(1, row_size)
    ]
    raw = lead_rows(capacity, first, lead)

    steps = range(2, half, 2)
    across = lax.ppermute(raw, "col", across_col(half))
    inner = [lax.ppermute(raw, "col", across_col(k)) for k in steps]
    near = [send_edge(k, lax.optimization_barrier((edge[k], raw))[0]) for k in range(1, half)]
    arrived.append(exchange(second, arrived[0], across, *inner, *near))
    outer = [lax.ppermute(across, "col", across_col(k)) for k in steps]
    known = [raw, *inner, across]
    beside = lax.ppermute(jnp.stack(known), "col", across_col(1))
    outside = lax.ppermute(jnp.stack(outer), "col", across_col(1))
    raw_rows = order_rows(ids, known + outer, jnp.concatenate([beside, outside]))
    arrived.append(exchange(packed(parts[2], across), arrived[1], beside, outside))
    edge = [edge[0], *near, *far]

    *moved, _ = lax.optimization_barrier((*moved, raw))
    kids = jnp.concatenate(
        [moved[0]]
        + [lax.ppermute(moved[shift], "row", along_row(shift)) for shift in range(1, row_size)]
    )

    corner_mine = corner = raw_rows[:, 0].reshape(width, width)
    corner = jnp.where(my_row == 0, corner, 0.0)
    for shift in range(1, row_size):
        corner = corner + lax.ppermute(corner_mine, "row", [(0, shift)])
    corner = 0.5 * (corner + corner.T)
    factor, inverse = factor_and_inverse(corner)

    mine = lax.dynamic_index_in_dim(
        raw_rows.reshape(col_size, col_tiles, group, chunk, width),
        my_col // row_size,
        2,
        keepdims=False,
    )
    raw_cols = jnp.where(my_row == my_col % row_size, mine, 0.0)
    for shift in range(1, row_size):
        steps = [
            ((c % row_size) * col_size + c, ((c + shift) % row_size) * col_size + c)
            for c in range(col_size)
        ]
        raw_cols = raw_cols + lax.ppermute(mine, ("row", "col"), steps)
    rows, high, low = panels(ids, inverse, factor, raw_rows, raw_cols)

    out = None
    for step, part in enumerate(parts):
        if step == 2:
            arrived.append(exchange(packed(parts[3]), arrived[2], out))
        out = finish(
            part,
            [shared[a] for a in part],
            [edge_of.get(a) for a in part],
            row_size,
            col_size,
            ids,
            own,
            arrived[step],
            rows,
            high,
            low,
            kids,
            edge,
            out,
        )
    return out.reshape(row_tiles, 1, width, col_tiles, 1, width)


def solution(mesh):
    return jax.shard_map(
        on_device,
        mesh=mesh,
        in_specs=(
            P(None, "row", "col", None, None, None),
            P("row", "col", None, None, None),
            P("row", "col", None),
            P("row", "col", None),
            P("row", "col"),
            P("row", "col", None, None),
            P("row", "col", None, None),
        ),
        out_specs=P(None, "row", None, None, "col", None),
        check_vma=False,
    )
```

```python
import functools

import jax
import jax.numpy as jnp
from jax import lax
from jax.experimental import pallas as pl
from jax.experimental.pallas import tpu as pltpu
from jax.sharding import PartitionSpec as P

HIGHEST = lax.Precision.HIGHEST
LANES = 128
VMEM_LIMIT = 60 << 20


def bf16_nt(left, right):
    return lax.dot_general(
        left, right, (((1,), (1,)), ((), ())), preferred_element_type=jnp.float32
    )


def depth_blocks(a, row_size, col_size):
    return (a * row_size + row_size - 1) // col_size + 1


def shared_blocks(a, row_size, col_size):
    return (a * row_size + row_size - 1 - col_size // 2) // col_size + 1


def move_kernel(
    row_size,
    capacity,
    ids_ref,
    rows_ref,
    cols_ref,
    count_ref,
    tiles_ref,
    row_map_ref,
    col_map_ref,
    *out_refs,
):
    slots, width = tiles_ref.shape[0], tiles_ref.shape[1]
    out_refs, lead_refs = out_refs[:row_size], out_refs[row_size:]
    chunk = width // (2 * len(lead_refs))
    labels = lax.broadcasted_iota(jnp.int32, (width, width), 0)
    count = count_ref[0]

    def one(shift, place, out_ref):
        owner = lax.rem(ids_ref[0] + shift, row_size)
        def scan(k, state):
            chosen, seen = state
            hit = (lax.rem(rows_ref[k], row_size) == owner) & (k < count)
            chosen = jnp.where(hit & (seen == place), k, chosen)
            return chosen, seen + hit.astype(jnp.int32)

        chosen, seen = lax.fori_loop(0, slots, scan, (jnp.int32(0), jnp.int32(0)))
        row_hot = (labels == row_map_ref[pl.ds(chosen, 1), :]).astype(jnp.bfloat16)
        col_hot = (labels == col_map_ref[pl.ds(chosen, 1), :]).astype(jnp.bfloat16)
        left = tiles_ref[chosen]
        tile = None
        for _ in range(3):
            term = left.astype(jnp.bfloat16)
            left = left - term.astype(jnp.float32)
            moved = jnp.dot(row_hot, term, preferred_element_type=jnp.float32)
            moved = bf16_nt(moved.astype(jnp.bfloat16), col_hot)
            tile = moved if tile is None else tile + moved
        out_ref[place] = tile
        here = (seen > place) & (cols_ref[chosen] == 0)
        target = jnp.where(here, rows_ref[chosen] // row_size, -1).astype(jnp.float32)
        mark = jnp.full((1, width), target)
        for pair, lead_ref in enumerate(lead_refs):
            for side in range(2):
                first = (2 * pair + side) * chunk
                lead_ref[side, shift, pl.ds(place * chunk, chunk), :] = tile[first : first + chunk]
                lead_ref[side, shift, pl.ds(capacity * chunk + place, 1), :] = mark

    for shift, out_ref in enumerate(out_refs):
        for place in range(capacity):
            one(shift, place, out_ref)


def move_tiles(row_size, col_size, capacity, ids, rows, cols, count, tiles, row_maps, col_maps):
    slots, width = tiles.shape[0], tiles.shape[1]
    smem = pl.BlockSpec(memory_space=pltpu.SMEM)
    vmem = pl.BlockSpec(memory_space=pltpu.VMEM)
    return pl.pallas_call(
        functools.partial(move_kernel, row_size, capacity),
        out_shape=[jax.ShapeDtypeStruct((capacity, width, width), jnp.float32)] * row_size
        + [
            jax.ShapeDtypeStruct(
                (2, row_size, capacity * (width // col_size) + 8, width), jnp.float32
            )
        ]
        * (col_size // 2),
        in_specs=[smem, smem, smem, smem, vmem, vmem, vmem],
        out_specs=[vmem] * (row_size + col_size // 2),
        compiler_params=pltpu.CompilerParams(vmem_limit_bytes=VMEM_LIMIT),
        name="move_tiles",
    )(ids, rows, cols, count, tiles, row_maps, col_maps)


def locate_kernel(row_size, capacity, slots, ids_ref, meta_ref, own_ref):
    my_row = ids_ref[0]

    def clear(n, carry):
        own_ref[0, n] = -1
        own_ref[1, n] = -1
        return carry

    lax.fori_loop(0, row_size * capacity, clear, 0)

    def source(s, carry):
        line = lax.rem(my_row + row_size - s, row_size)
        count = meta_ref[line, 2 * slots]

        def slot(k, seen):
            target = meta_ref[line, k]
            hit = (lax.rem(target, row_size) == my_row) & (k < count)

            @pl.when(hit)
            def _():
                own_ref[0, s * capacity + seen] = target // row_size
                own_ref[1, s * capacity + seen] = meta_ref[line, slots + k]

            return jnp.minimum(seen + hit.astype(jnp.int32), capacity - 1)

        lax.fori_loop(0, slots, slot, jnp.int32(0))
        return carry

    lax.fori_loop(0, row_size, source, 0)


def locate(row_size, capacity, slots, ids, meta):
    smem = pl.BlockSpec(memory_space=pltpu.SMEM)
    return pl.pallas_call(
        functools.partial(locate_kernel, row_size, capacity, slots),
        out_shape=jax.ShapeDtypeStruct((2, row_size * capacity), jnp.int32),
        in_specs=[smem, smem],
        out_specs=smem,
        name="locate",
    )(ids, meta)


def first_kernel(front_ref, out_ref, buf, sem):
    row_tiles, chunk, col_size = front_ref.shape[0], front_ref.shape[2], front_ref.shape[4]
    copies = [
        pltpu.make_async_copy(
            front_ref.at[:, 0, :, 0, :, pl.ds(half * LANES, LANES)], buf.at[half], sem.at[half]
        )
        for half in range(2)
    ]
    for copy in copies:
        copy.start()
    for copy in copies:
        copy.wait()
    for half in range(2):
        flat = buf.at[half].reshape(row_tiles * chunk * col_size, LANES)
        for a in range(row_tiles):
            out_ref[a, :, half * LANES : (half + 1) * LANES] = flat[
                pl.ds(a * chunk * col_size, chunk, stride=col_size), :
            ]


def first_rows(front):
    row_tiles, chunk, col_size, width = front.shape[0], front.shape[2], front.shape[4], front.shape[5]
    return pl.pallas_call(
        first_kernel,
        out_shape=jax.ShapeDtypeStruct((row_tiles, chunk, width), jnp.float32),
        in_specs=[pl.BlockSpec(memory_space=pltpu.HBM)],
        out_specs=pl.BlockSpec(memory_space=pltpu.VMEM),
        scratch_shapes=[
            pltpu.VMEM((2, row_tiles, chunk, col_size, LANES), jnp.float32),
            pltpu.SemaphoreType.DMA((2,)),
        ],
        compiler_params=pltpu.CompilerParams(vmem_limit_bytes=VMEM_LIMIT),
        name="first_rows",
    )(front)


def lead_kernel(capacity, own_ref, *refs):
    kids_refs, out_ref = refs[:-1], refs[-1]
    chunk = own_ref.shape[1]

    def one(a, carry):
        total = own_ref[a]
        for kids_ref in kids_refs:
            for place in range(capacity):
                kid = kids_ref[pl.ds(place * chunk, chunk), :]
                target = kids_ref[pl.ds(capacity * chunk + place, 1), :]
                total += jnp.where(target == a.astype(jnp.float32), kid, 0.0)
        out_ref[a] = total
        return carry

    lax.fori_loop(0, own_ref.shape[0], one, 0)


def lead_rows(capacity, own, kids):
    vmem = pl.BlockSpec(memory_space=pltpu.VMEM)
    return pl.pallas_call(
        functools.partial(lead_kernel, capacity),
        out_shape=jax.ShapeDtypeStruct(own.shape, jnp.float32),
        in_specs=[vmem] * (1 + len(kids)),
        out_specs=vmem,
        compiler_params=pltpu.CompilerParams(vmem_limit_bytes=VMEM_LIMIT),
        name="lead_rows",
    )(own, *kids)


def order_kernel(ids_ref, *refs):
    same, other_ref, out_ref = refs[:-2], refs[-2], refs[-1]
    for k, same_ref in enumerate(same):
        out_ref[lax.bitwise_xor(ids_ref[1], 2 * k)] = same_ref[...]
        out_ref[lax.bitwise_xor(ids_ref[1], 2 * k + 1)] = other_ref[k]


def order_rows(ids, same, other):
    smem = pl.BlockSpec(memory_space=pltpu.SMEM)
    vmem = pl.BlockSpec(memory_space=pltpu.VMEM)
    return pl.pallas_call(
        order_kernel,
        out_shape=jax.ShapeDtypeStruct((2 * len(same),) + same[0].shape, jnp.float32),
        in_specs=[smem] + [vmem] * (1 + len(same)),
        out_specs=vmem,
        compiler_params=pltpu.CompilerParams(vmem_limit_bytes=VMEM_LIMIT),
        name="order_rows",
    )(ids, *same, other)


def halves_of(value):
    high = value.astype(jnp.bfloat16)
    return high, (value - high.astype(jnp.float32)).astype(jnp.bfloat16)


def panel_kernel(ids_ref, inverse_ref, factor_ref, rows_ref, cols_ref, row_out, high_out, low_out):
    width = inverse_ref.shape[0]
    high, low = halves_of(inverse_ref[...])

    def solve(tile):
        tile_high, tile_low = halves_of(tile)
        return bf16_nt(tile_high, high) + (bf16_nt(tile_high, low) + bf16_nt(tile_low, high))

    def row(a, carry):
        row_out[a] = solve(rows_ref[:, a].reshape(width, width))
        return carry

    lax.fori_loop(0, row_out.shape[0], row, 0)

    @pl.when(ids_ref[0] == 0)
    def _():
        row_out[0] = factor_ref[...]

    def column(b, carry):
        col = solve(cols_ref[:, b].reshape(width, width))
        high_out[b], low_out[b] = halves_of(col)
        return carry

    lax.fori_loop(0, high_out.shape[0], column, 0)


def panels(ids, inverse, factor, rows, cols):
    smem = pl.BlockSpec(memory_space=pltpu.SMEM)
    vmem = pl.BlockSpec(memory_space=pltpu.VMEM)
    width = inverse.shape[0]
    return pl.pallas_call(
        panel_kernel,
        out_shape=(
            jax.ShapeDtypeStruct((rows.shape[1], width, width), jnp.float32),
            jax.ShapeDtypeStruct((cols.shape[1], width, width), jnp.bfloat16),
            jax.ShapeDtypeStruct((cols.shape[1], width, width), jnp.bfloat16),
        ),
        in_specs=[smem, vmem, vmem, vmem, vmem],
        out_specs=(vmem, vmem, vmem),
        compiler_params=pltpu.CompilerParams(vmem_limit_bytes=VMEM_LIMIT),
        name="panels",
    )(ids, inverse, factor, rows, cols)


def pack_kernel(depths, counts, front_ref, out_ref, in_buf, out_buf, in_sem, out_sem):
    col_size = front_ref.shape[4]
    chunk = front_ref.shape[2]

    def fetch(i):
        a, nb, slot = depths[i], counts[i], i % 2
        return [
            pltpu.make_async_copy(
                front_ref.at[a, 0, :, pl.ds(0, nb), :, pl.ds(half * LANES, LANES)],
                in_buf.at[slot, half, :, pl.ds(0, nb)],
                in_sem.at[slot, half],
            )
            for half in range(2)
        ]

    def send(i):
        first, nb, slot = sum(counts[:i]), counts[i], i % 2
        return pltpu.make_async_copy(
            out_buf.at[slot, :, pl.ds(0, nb)], out_ref.at[:, pl.ds(first, nb)], out_sem.at[slot]
        )

    steps = len(depths)
    for copy in fetch(0):
        copy.start()
    for i in range(steps):
        slot, nb = i % 2, counts[i]
        if i + 1 < steps:
            for copy in fetch(i + 1):
                copy.start()
        for copy in fetch(i):
            copy.wait()
        if i >= 2:
            send(i - 2).wait()
        for half in range(2):
            total = in_buf.shape[3]
            flat = in_buf.at[slot, half].reshape(chunk * total * col_size, LANES)
            for b in range(nb):
                for c in range(col_size):
                    out_buf[slot, c, b, :, half * LANES : (half + 1) * LANES] = flat[
                        pl.ds(b * col_size + c, chunk, stride=total * col_size), :
                    ]
        send(i).start()
    for i in range(max(steps - 2, 0), steps):
        send(i).wait()


def pack(front, depths, counts):
    chunk, col_size, width = front.shape[2], front.shape[4], front.shape[5]
    most = max(counts)
    return pl.pallas_call(
        functools.partial(pack_kernel, depths, counts),
        out_shape=jax.ShapeDtypeStruct((col_size, sum(counts), chunk, width), jnp.float32),
        in_specs=[pl.BlockSpec(memory_space=pltpu.HBM)],
        out_specs=pl.BlockSpec(memory_space=pltpu.HBM),
        scratch_shapes=[
            pltpu.VMEM((2, 2, chunk, most, col_size, LANES), jnp.float32),
            pltpu.VMEM((2, col_size, most, chunk, width), jnp.float32),
            pltpu.SemaphoreType.DMA((2, 2)),
            pltpu.SemaphoreType.DMA((2,)),
        ],
        compiler_params=pltpu.CompilerParams(vmem_limit_bytes=VMEM_LIMIT),
        name="pack",
    )(front)


def edge_kernel(blocks, ids_ref, front_ref, *refs):
    out_refs, (buf, sem) = refs[:-2], refs[-2:]
    chunk, col_size = front_ref.shape[2], front_ref.shape[4]
    copies = [
        pltpu.make_async_copy(
            front_ref.at[a, 0, :, b, :, pl.ds(half * LANES, LANES)], buf.at[i, half], sem.at[i, half]
        )
        for i, (a, b) in enumerate(blocks)
        for half in range(2)
    ]
    for copy in copies:
        copy.start()
    for copy in copies:
        copy.wait()
    for i in range(len(blocks)):
        for half in range(2):
            flat = buf.at[i, half].reshape(chunk * col_size, LANES)
            for k, out_ref in enumerate(out_refs):
                out_ref[i, :, half * LANES : (half + 1) * LANES] = flat[
                    pl.ds(lax.bitwise_xor(ids_ref[1], k), chunk, stride=col_size), :
                ]


def pack_edge(ids, front, blocks):
    chunk, col_size, width = front.shape[2], front.shape[4], front.shape[5]
    vmem = pl.BlockSpec(memory_space=pltpu.VMEM)
    return pl.pallas_call(
        functools.partial(edge_kernel, blocks),
        out_shape=[jax.ShapeDtypeStruct((len(blocks), chunk, width), jnp.float32)] * col_size,
        in_specs=[pl.BlockSpec(memory_space=pltpu.SMEM), pl.BlockSpec(memory_space=pltpu.HBM)],
        out_specs=[vmem] * col_size,
        scratch_shapes=[
            pltpu.VMEM((len(blocks), 2, chunk, col_size, LANES), jnp.float32),
            pltpu.SemaphoreType.DMA((len(blocks), 2)),
        ],
        compiler_params=pltpu.CompilerParams(vmem_limit_bytes=VMEM_LIMIT),
        name="pack_edge",
    )(ids, front)


def finish_kernel(
    depths,
    shared,
    edges,
    row_size,
    col_size,
    ids_ref,
    own_ref,
    recv_ref,
    rows_ref,
    high_ref,
    low_ref,
    kids_ref,
    *rest,
):
    edge_refs = rest[:col_size]
    out_ref, in_buf, row_buf, out_buf, high_buf, low_buf, kid_buf, *sems = rest[-13:]
    in_sem, row_sem, out_sem, col_sem, kid_sem, edge_sem = sems
    my_row, my_col = ids_ref[0], ids_ref[1]
    width = high_ref.shape[1]
    chunk = width // col_size
    halves = width // LANES
    blocks = high_ref.shape[0]
    stride = blocks * halves

    counts = [n + (edge is not None) for n, edge in zip(shared, edges)]

    def fetch(i):
        a, nb, edge, slot, first = depths[i], shared[i], edges[i], i % 2, sum(shared[:i])
        copies = [pltpu.make_async_copy(rows_ref.at[a], row_buf.at[slot], row_sem.at[slot])]
        if nb:
            copies.append(
                pltpu.make_async_copy(
                    recv_ref.at[:, pl.ds(first, nb)],
                    in_buf.at[slot, :, pl.ds(0, nb)],
                    in_sem.at[slot],
                )
            )
        if edge is not None:
            for k, edge_ref in enumerate(edge_refs):
                copies.append(
                    pltpu.make_async_copy(
                        edge_ref.at[edge],
                        in_buf.at[slot, lax.bitwise_xor(my_col, k), nb],
                        edge_sem.at[slot, k],
                    )
                )
        return copies

    def send(i):
        return pltpu.make_async_copy(out_buf.at[i % 2], out_ref.at[depths[i]], out_sem.at[i % 2])

    most = high_buf.shape[0]
    columns = [
        pltpu.make_async_copy(high_ref.at[pl.ds(0, most)], high_buf, col_sem.at[0]),
        pltpu.make_async_copy(low_ref.at[pl.ds(0, most)], low_buf, col_sem.at[1]),
    ]
    steps = len(depths)
    for copy in (*fetch(0), *columns):
        copy.start()
    for i in range(steps):
        a, nb, slot = depths[i], counts[i], i % 2
        if i + 1 < steps:
            for copy in fetch(i + 1):
                copy.start()
        for copy in fetch(i):
            copy.wait()
        if i == 0:
            for copy in columns:
                copy.wait()
        if i >= 2:
            send(i - 2).wait()
        for n in range(kids_ref.shape[0]):

            @pl.when(own_ref[0, n] == a)
            def _():
                copy = pltpu.make_async_copy(kids_ref.at[n], kid_buf, kid_sem)
                copy.start()
                copy.wait()
                in_buf[slot, :, own_ref[1, n]] += kid_buf[...].reshape(col_size, chunk, width)

        tile_i = a * row_size + my_row

        def store(b, tile):
            for half in range(halves):
                out_buf[slot, pl.ds(b * halves + half, width, stride=stride), :] = tile[
                    :, half * LANES : (half + 1) * LANES
                ]

        row_high, row_low = halves_of(row_buf[slot])

        def update(b):
            return bf16_nt(row_high, high_buf[b]) + (
                bf16_nt(row_high, low_buf[b]) + bf16_nt(row_low, high_buf[b])
            )

        for b in range(nb):
            tile = in_buf[slot, :, b].reshape(width, width)
            tile_j = b * col_size + my_col
            if b < nb - 1:
                store(b, tile - update(b))
            else:

                @pl.when(tile_i > tile_j)
                def _():
                    store(b, tile - update(b))

                @pl.when(tile_i == tile_j)
                def _():
                    store(b, 0.5 * (tile + tile.T) - update(b))

                @pl.when(tile_i < tile_j)
                def _():
                    store(b, jnp.zeros_like(tile))

        @pl.when(my_col == 0)
        def _():
            store(0, row_buf[slot])

        zero = jnp.zeros((width, LANES), jnp.float32)
        for n in range(nb * halves, stride):
            out_buf[slot, pl.ds(n, width, stride=stride), :] = zero
        send(i).start()
    for i in range(max(steps - 2, 0), steps):
        send(i).wait()


def finish(
    depths, shared, edges, row_size, col_size, ids, own, recv, rows, high, low, kids, edge, out=None
):
    smem = pl.BlockSpec(memory_space=pltpu.SMEM)
    hbm = pl.BlockSpec(memory_space=pltpu.HBM)
    blocks, width = high.shape[0], high.shape[1]
    chunk = width // col_size
    lines = width * blocks * (width // LANES)
    counts = [n + (edge is not None) for n, edge in zip(shared, edges)]
    operands = [ids, own, recv, rows, high, low, kids, *edge]
    in_specs = [smem, smem] + [hbm] * (5 + len(edge))
    aliases = {}
    if out is not None:
        operands.append(out)
        in_specs.append(hbm)
        aliases = {len(operands) - 1: 0}
    return pl.pallas_call(
        functools.partial(finish_kernel, depths, shared, edges, row_size, col_size),
        out_shape=jax.ShapeDtypeStruct((rows.shape[0], lines, LANES), jnp.float32),
        in_specs=in_specs,
        out_specs=hbm,
        scratch_shapes=[
            pltpu.VMEM((2, col_size, max(counts), chunk, width), jnp.float32),
            pltpu.VMEM((2, width, width), jnp.float32),
            pltpu.VMEM((2, lines, LANES), jnp.float32),
            pltpu.VMEM((max(counts), width, width), jnp.bfloat16),
            pltpu.VMEM((max(counts), width, width), jnp.bfloat16),
            pltpu.VMEM((width, width), jnp.float32),
            pltpu.SemaphoreType.DMA((2,)),
            pltpu.SemaphoreType.DMA((2,)),
            pltpu.SemaphoreType.DMA((2,)),
            pltpu.SemaphoreType.DMA((2,)),
            pltpu.SemaphoreType.DMA,
            pltpu.SemaphoreType.DMA((2, col_size)),
        ],
        input_output_aliases=aliases,
        compiler_params=pltpu.CompilerParams(vmem_limit_bytes=VMEM_LIMIT),
        name="finish",
    )(*operands)


def factor_and_inverse(corner):
    size = corner.shape[0] // 2
    eye = jnp.eye(size, dtype=jnp.float32)

    def both(block):
        factor = lax.linalg.cholesky(block, symmetrize_input=False)
        return factor, jax.scipy.linalg.solve_triangular(factor, eye, lower=True)

    def product(left, right):
        return jnp.dot(left, right, precision=HIGHEST)

    top, top_inverse = both(corner[:size, :size])
    below = product(corner[size:, :size], top_inverse.T)
    end, end_inverse = both(corner[size:, size:] - product(below, below.T))
    corner_inverse = -product(end_inverse, product(below, top_inverse))
    zero = jnp.zeros_like(eye)
    return (
        jnp.block([[top, zero], [below, end]]),
        jnp.block([[top_inverse, zero], [corner_inverse, end_inverse]]),
    )


def on_device(front, child_tiles, child_rows, child_cols, child_counts, row_maps, col_maps):
    row_size, col_size = lax.axis_size("row"), lax.axis_size("col")
    my_row, my_col = lax.axis_index("row"), lax.axis_index("col")
    row_tiles, chunk, col_tiles, width = front.shape[0], front.shape[2], front.shape[3], front.shape[5]
    slots = child_tiles.shape[2]
    capacity = slots // 4
    arrivals = row_size * capacity
    group = col_size // row_size
    ids = jnp.stack([my_row, my_col]).astype(jnp.int32)

    shared = [shared_blocks(a, row_size, col_size) for a in range(row_tiles)]
    edge_blocks = [
        (a, shared[a]) for a in range(row_tiles) if depth_blocks(a, row_size, col_size) > shared[a]
    ]
    edge_of = {a: i for i, (a, _) in enumerate(edge_blocks)}
    last = (row_tiles - 5) * 3 // 4 + 1
    parts = [[row_tiles - 2], [row_tiles - 1, row_tiles - 3, row_tiles - 4]]
    parts.append([a for a in range(row_tiles - 5, -1, -1) if a != last])
    parts.append([last])

    def packed(part, *after):
        held = lax.optimization_barrier((front,) + after)[0]
        sent = [a for a in part if shared[a]]
        return pack(held, sent, [shared[a] for a in sent])

    def exchange(blocks, *after):
        blocks = lax.optimization_barrier((blocks,) + after)[0]
        return lax.all_to_all(blocks, "col", split_axis=0, concat_axis=0, tiled=True)

    def along_row(shift):
        return [(r, (r + shift) % row_size) for r in range(row_size)]

    def across_col(k):
        return [(c, c ^ k) for c in range(col_size)]

    moved = move_tiles(
        row_size,
        col_size,
        capacity,
        ids,
        child_rows.reshape(slots),
        child_cols.reshape(slots),
        child_counts.reshape(1),
        child_tiles.reshape(slots, width, width),
        row_maps.reshape(slots, width),
        col_maps.reshape(slots, width),
    )
    moved, pieces = moved[:row_size], moved[row_size:]

    sent = [
        lax.ppermute(pieces[pair], "col", [(0, 2 * pair)]) for pair in range(1, col_size // 2)
    ]
    edge = pack_edge(ids, lax.optimization_barrier((front, pieces[0]))[0], edge_blocks)

    def send_edge(k, value):
        steps = [
            (r * col_size + c, r * col_size + (c ^ k))
            for r in range(row_size)
            for c in range(col_size)
            if c ^ k <= r
        ]
        return lax.ppermute(value, ("row", "col"), steps)

    half = col_size // 2
    far = [send_edge(k, edge[k]) for k in range(half, col_size)]
    second = packed(parts[1], pieces[0])
    blocks = packed(parts[0], pieces[0])
    first = first_rows(front)
    *sent, blocks, _ = lax.optimization_barrier((*sent, blocks, *far[:1]))
    arrived = [exchange(blocks, *sent, *far)]
    lead = jnp.where(my_col == 0, pieces[0], sum(sent[1:], sent[0]))
    other = lax.ppermute(lead[1], "col", [(c, c + 1) for c in range(0, col_size, 2)])
    other, second, first = lax.optimization_barrier((other, second, first))
    lead = jnp.where(my_col % 2 == 0, lead[0], other)
    lead = [lead[0]] + [
        lax.ppermute(lead[shift], "row", along_row(shift)) for shift in range(1, row_size)
    ]
    raw = lead_rows(capacity, first, lead)

    steps = range(2, half, 2)
    across = lax.ppermute(raw, "col", across_col(half))
    inner = [lax.ppermute(raw, "col", across_col(k)) for k in steps]
    near = [send_edge(k, lax.optimization_barrier((edge[k], raw))[0]) for k in range(1, half)]
    arrived.append(exchange(second, arrived[0], across, *inner, *near))
    outer = [lax.ppermute(across, "col", across_col(k)) for k in steps]
    known = [raw, *inner, across]
    third = packed(parts[2], across)
    stacked, third = lax.optimization_barrier((jnp.stack(known), third))
    beside = lax.ppermute(stacked, "col", across_col(1))
    outside = lax.ppermute(jnp.stack(outer), "col", across_col(1))
    raw_rows = order_rows(ids, known + outer, jnp.concatenate([beside, outside]))
    meta = jnp.concatenate(
        [child_rows.reshape(1, slots), child_cols.reshape(1, slots), child_counts.reshape(1, 1)], axis=1
    )
    meta, _ = lax.optimization_barrier((meta, across))
    meta = lax.all_gather(meta, "row", axis=0, tiled=True)
    own = locate(row_size, capacity, slots, ids, meta)
    *moved, _ = lax.optimization_barrier((*moved, across))
    kids = jnp.concatenate(
        [moved[0]]
        + [lax.ppermute(moved[shift], "row", along_row(shift)) for shift in range(1, row_size)]
    )

    arrived.append(exchange(third, arrived[1], beside, outside, own, kids))
    edge = [edge[0], *near, *far]

    corner_mine = corner = raw_rows[:, 0].reshape(width, width)
    corner = jnp.where(my_row == 0, corner, 0.0)
    for shift in range(1, row_size):
        corner = corner + lax.ppermute(corner_mine, "row", [(0, shift)])
    corner = 0.5 * (corner + corner.T)
    factor, inverse = factor_and_inverse(corner)

    mine = lax.dynamic_index_in_dim(
        raw_rows.reshape(col_size, col_tiles, group, chunk, width),
        my_col // row_size,
        2,
        keepdims=False,
    )
    raw_cols = jnp.where(my_row == my_col % row_size, mine, 0.0)
    for shift in range(1, row_size):
        steps = [
            ((c % row_size) * col_size + c, ((c + shift) % row_size) * col_size + c)
            for c in range(col_size)
        ]
        raw_cols = raw_cols + lax.ppermute(mine, ("row", "col"), steps)
    rows, high, low = panels(ids, inverse, factor, raw_rows, raw_cols)

    out = None
    for step, part in enumerate(parts):
        if step == 2:
            arrived.append(exchange(packed(parts[3]), arrived[2], out))
        out = finish(
            part,
            [shared[a] for a in part],
            [edge_of.get(a) for a in part],
            row_size,
            col_size,
            ids,
            own,
            arrived[step],
            rows,
            high,
            low,
            kids,
            edge,
            out,
        )
    return out.reshape(row_tiles, 1, width, col_tiles, 1, width)


def solution(mesh):
    return jax.shard_map(
        on_device,
        mesh=mesh,
        in_specs=(
            P(None, "row", "col", None, None, None),
            P("row", "col", None, None, None),
            P("row", "col", None),
            P("row", "col", None),
            P("row", "col"),
            P("row", "col", None, None),
            P("row", "col", None, None),
        ),
        out_specs=P(None, "row", None, None, "col", None),
        check_vma=False,
    )
```

```python
import functools

import jax
import jax.numpy as jnp
from jax import lax
from jax.experimental import pallas as pl
from jax.experimental.pallas import tpu as pltpu
from jax.sharding import PartitionSpec as P

HIGHEST = lax.Precision.HIGHEST
LANES = 128
VMEM_LIMIT = 60 << 20


def bf16_nt(left, right):
    return lax.dot_general(
        left, right, (((1,), (1,)), ((), ())), preferred_element_type=jnp.float32
    )


def depth_blocks(a, row_size, col_size):
    return (a * row_size + row_size - 1) // col_size + 1


def shared_blocks(a, row_size, col_size):
    return (a * row_size + row_size - 1 - col_size // 2) // col_size + 1


def move_kernel(
    row_size,
    capacity,
    ids_ref,
    rows_ref,
    cols_ref,
    count_ref,
    tiles_ref,
    row_map_ref,
    col_map_ref,
    *out_refs,
):
    slots, width = tiles_ref.shape[0], tiles_ref.shape[1]
    out_refs, lead_refs = out_refs[:row_size], out_refs[row_size:]
    chunk = width // (2 * len(lead_refs))
    labels = lax.broadcasted_iota(jnp.int32, (width, width), 0)
    count = count_ref[0]

    def one(shift, place, out_ref):
        owner = lax.rem(ids_ref[0] + shift, row_size)
        def scan(k, state):
            chosen, seen = state
            hit = (lax.rem(rows_ref[k], row_size) == owner) & (k < count)
            chosen = jnp.where(hit & (seen == place), k, chosen)
            return chosen, seen + hit.astype(jnp.int32)

        chosen, seen = lax.fori_loop(0, slots, scan, (jnp.int32(0), jnp.int32(0)))
        row_hot = (labels == row_map_ref[pl.ds(chosen, 1), :]).astype(jnp.bfloat16)
        col_hot = (labels == col_map_ref[pl.ds(chosen, 1), :]).astype(jnp.bfloat16)
        left = tiles_ref[chosen]
        tile = None
        for _ in range(3):
            term = left.astype(jnp.bfloat16)
            left = left - term.astype(jnp.float32)
            moved = jnp.dot(row_hot, term, preferred_element_type=jnp.float32)
            moved = bf16_nt(moved.astype(jnp.bfloat16), col_hot)
            tile = moved if tile is None else tile + moved
        out_ref[place] = tile
        here = (seen > place) & (cols_ref[chosen] == 0)
        target = jnp.where(here, rows_ref[chosen] // row_size, -1).astype(jnp.float32)
        mark = jnp.full((1, width), target)
        for pair, lead_ref in enumerate(lead_refs):
            for side in range(2):
                first = (2 * pair + side) * chunk
                lead_ref[side, shift, pl.ds(place * chunk, chunk), :] = tile[first : first + chunk]
                lead_ref[side, shift, pl.ds(capacity * chunk + place, 1), :] = mark

    for shift, out_ref in enumerate(out_refs):
        for place in range(capacity):
            one(shift, place, out_ref)


def move_tiles(row_size, col_size, capacity, ids, rows, cols, count, tiles, row_maps, col_maps):
    slots, width = tiles.shape[0], tiles.shape[1]
    smem = pl.BlockSpec(memory_space=pltpu.SMEM)
    vmem = pl.BlockSpec(memory_space=pltpu.VMEM)
    return pl.pallas_call(
        functools.partial(move_kernel, row_size, capacity),
        out_shape=[jax.ShapeDtypeStruct((capacity, width, width), jnp.float32)] * row_size
        + [
            jax.ShapeDtypeStruct(
                (2, row_size, capacity * (width // col_size) + 8, width), jnp.float32
            )
        ]
        * (col_size // 2),
        in_specs=[smem, smem, smem, smem, vmem, vmem, vmem],
        out_specs=[vmem] * (row_size + col_size // 2),
        compiler_params=pltpu.CompilerParams(vmem_limit_bytes=VMEM_LIMIT),
        name="move_tiles",
    )(ids, rows, cols, count, tiles, row_maps, col_maps)


def locate_kernel(row_size, capacity, slots, ids_ref, meta_ref, own_ref):
    my_row = ids_ref[0]

    def clear(n, carry):
        own_ref[0, n] = -1
        own_ref[1, n] = -1
        return carry

    lax.fori_loop(0, row_size * capacity, clear, 0)

    def source(s, carry):
        line = lax.rem(my_row + row_size - s, row_size)
        count = meta_ref[line, 2 * slots]

        def slot(k, seen):
            target = meta_ref[line, k]
            hit = (lax.rem(target, row_size) == my_row) & (k < count)

            @pl.when(hit)
            def _():
                own_ref[0, s * capacity + seen] = target // row_size
                own_ref[1, s * capacity + seen] = meta_ref[line, slots + k]

            return jnp.minimum(seen + hit.astype(jnp.int32), capacity - 1)

        lax.fori_loop(0, slots, slot, jnp.int32(0))
        return carry

    lax.fori_loop(0, row_size, source, 0)


def locate(row_size, capacity, slots, ids, meta):
    smem = pl.BlockSpec(memory_space=pltpu.SMEM)
    return pl.pallas_call(
        functools.partial(locate_kernel, row_size, capacity, slots),
        out_shape=jax.ShapeDtypeStruct((2, row_size * capacity), jnp.int32),
        in_specs=[smem, smem],
        out_specs=smem,
        name="locate",
    )(ids, meta)


def first_kernel(front_ref, out_ref, buf, sem):
    row_tiles, chunk, col_size = front_ref.shape[0], front_ref.shape[2], front_ref.shape[4]
    copies = [
        pltpu.make_async_copy(
            front_ref.at[:, 0, :, 0, :, pl.ds(half * LANES, LANES)], buf.at[half], sem.at[half]
        )
        for half in range(2)
    ]
    for copy in copies:
        copy.start()
    for copy in copies:
        copy.wait()
    for half in range(2):
        flat = buf.at[half].reshape(row_tiles * chunk * col_size, LANES)
        for a in range(row_tiles):
            out_ref[a, :, half * LANES : (half + 1) * LANES] = flat[
                pl.ds(a * chunk * col_size, chunk, stride=col_size), :
            ]


def first_rows(front):
    row_tiles, chunk, col_size, width = front.shape[0], front.shape[2], front.shape[4], front.shape[5]
    return pl.pallas_call(
        first_kernel,
        out_shape=jax.ShapeDtypeStruct((row_tiles, chunk, width), jnp.float32),
        in_specs=[pl.BlockSpec(memory_space=pltpu.HBM)],
        out_specs=pl.BlockSpec(memory_space=pltpu.VMEM),
        scratch_shapes=[
            pltpu.VMEM((2, row_tiles, chunk, col_size, LANES), jnp.float32),
            pltpu.SemaphoreType.DMA((2,)),
        ],
        compiler_params=pltpu.CompilerParams(vmem_limit_bytes=VMEM_LIMIT),
        name="first_rows",
    )(front)


def lead_kernel(capacity, own_ref, *refs):
    kids_refs, out_ref = refs[:-1], refs[-1]
    chunk = own_ref.shape[1]

    def one(a, carry):
        total = own_ref[a]
        for kids_ref in kids_refs:
            for place in range(capacity):
                kid = kids_ref[pl.ds(place * chunk, chunk), :]
                target = kids_ref[pl.ds(capacity * chunk + place, 1), :]
                total += jnp.where(target == a.astype(jnp.float32), kid, 0.0)
        out_ref[a] = total
        return carry

    lax.fori_loop(0, own_ref.shape[0], one, 0)


def lead_rows(capacity, own, kids):
    vmem = pl.BlockSpec(memory_space=pltpu.VMEM)
    return pl.pallas_call(
        functools.partial(lead_kernel, capacity),
        out_shape=jax.ShapeDtypeStruct(own.shape, jnp.float32),
        in_specs=[vmem] * (1 + len(kids)),
        out_specs=vmem,
        compiler_params=pltpu.CompilerParams(vmem_limit_bytes=VMEM_LIMIT),
        name="lead_rows",
    )(own, *kids)


def order_kernel(ids_ref, *refs):
    same, other_ref, out_ref = refs[:-2], refs[-2], refs[-1]
    for k, same_ref in enumerate(same):
        out_ref[lax.bitwise_xor(ids_ref[1], 2 * k)] = same_ref[...]
        out_ref[lax.bitwise_xor(ids_ref[1], 2 * k + 1)] = other_ref[k]


def order_rows(ids, same, other):
    smem = pl.BlockSpec(memory_space=pltpu.SMEM)
    vmem = pl.BlockSpec(memory_space=pltpu.VMEM)
    return pl.pallas_call(
        order_kernel,
        out_shape=jax.ShapeDtypeStruct((2 * len(same),) + same[0].shape, jnp.float32),
        in_specs=[smem] + [vmem] * (1 + len(same)),
        out_specs=vmem,
        compiler_params=pltpu.CompilerParams(vmem_limit_bytes=VMEM_LIMIT),
        name="order_rows",
    )(ids, *same, other)


def halves_of(value):
    high = value.astype(jnp.bfloat16)
    return high, (value - high.astype(jnp.float32)).astype(jnp.bfloat16)


def panel_kernel(ids_ref, inverse_ref, factor_ref, rows_ref, cols_ref, row_out, high_out, low_out):
    width = inverse_ref.shape[0]
    high, low = halves_of(inverse_ref[...])

    def solve(tile):
        tile_high, tile_low = halves_of(tile)
        return bf16_nt(tile_high, high) + (bf16_nt(tile_high, low) + bf16_nt(tile_low, high))

    def row(a, carry):
        row_out[a] = solve(rows_ref[:, a].reshape(width, width))
        return carry

    lax.fori_loop(0, row_out.shape[0], row, 0)

    @pl.when(ids_ref[0] == 0)
    def _():
        row_out[0] = factor_ref[...]

    def column(b, carry):
        col = solve(cols_ref[:, b].reshape(width, width))
        high_out[b], low_out[b] = halves_of(col)
        return carry

    lax.fori_loop(0, high_out.shape[0], column, 0)


def panels(ids, inverse, factor, rows, cols):
    smem = pl.BlockSpec(memory_space=pltpu.SMEM)
    vmem = pl.BlockSpec(memory_space=pltpu.VMEM)
    width = inverse.shape[0]
    return pl.pallas_call(
        panel_kernel,
        out_shape=(
            jax.ShapeDtypeStruct((rows.shape[1], width, width), jnp.float32),
            jax.ShapeDtypeStruct((cols.shape[1], width, width), jnp.bfloat16),
            jax.ShapeDtypeStruct((cols.shape[1], width, width), jnp.bfloat16),
        ),
        in_specs=[smem, vmem, vmem, vmem, vmem],
        out_specs=(vmem, vmem, vmem),
        compiler_params=pltpu.CompilerParams(vmem_limit_bytes=VMEM_LIMIT),
        name="panels",
    )(ids, inverse, factor, rows, cols)


def pack_kernel(depths, counts, front_ref, out_ref, in_buf, out_buf, in_sem, out_sem):
    col_size = front_ref.shape[4]
    chunk = front_ref.shape[2]

    def fetch(i):
        a, nb, slot = depths[i], counts[i], i % 2
        return [
            pltpu.make_async_copy(
                front_ref.at[a, 0, :, pl.ds(0, nb), :, pl.ds(half * LANES, LANES)],
                in_buf.at[slot, half, :, pl.ds(0, nb)],
                in_sem.at[slot, half],
            )
            for half in range(2)
        ]

    def send(i):
        first, nb, slot = sum(counts[:i]), counts[i], i % 2
        return pltpu.make_async_copy(
            out_buf.at[slot, :, pl.ds(0, nb)], out_ref.at[:, pl.ds(first, nb)], out_sem.at[slot]
        )

    steps = len(depths)
    for copy in fetch(0):
        copy.start()
    for i in range(steps):
        slot, nb = i % 2, counts[i]
        if i + 1 < steps:
            for copy in fetch(i + 1):
                copy.start()
        for copy in fetch(i):
            copy.wait()
        if i >= 2:
            send(i - 2).wait()
        for half in range(2):
            total = in_buf.shape[3]
            flat = in_buf.at[slot, half].reshape(chunk * total * col_size, LANES)
            for b in range(nb):
                for c in range(col_size):
                    out_buf[slot, c, b, :, half * LANES : (half + 1) * LANES] = flat[
                        pl.ds(b * col_size + c, chunk, stride=total * col_size), :
                    ]
        send(i).start()
    for i in range(max(steps - 2, 0), steps):
        send(i).wait()


def pack(front, depths, counts):
    chunk, col_size, width = front.shape[2], front.shape[4], front.shape[5]
    most = max(counts)
    return pl.pallas_call(
        functools.partial(pack_kernel, depths, counts),
        out_shape=jax.ShapeDtypeStruct((col_size, sum(counts), chunk, width), jnp.float32),
        in_specs=[pl.BlockSpec(memory_space=pltpu.HBM)],
        out_specs=pl.BlockSpec(memory_space=pltpu.HBM),
        scratch_shapes=[
            pltpu.VMEM((2, 2, chunk, most, col_size, LANES), jnp.float32),
            pltpu.VMEM((2, col_size, most, chunk, width), jnp.float32),
            pltpu.SemaphoreType.DMA((2, 2)),
            pltpu.SemaphoreType.DMA((2,)),
        ],
        compiler_params=pltpu.CompilerParams(vmem_limit_bytes=VMEM_LIMIT),
        name="pack",
    )(front)


def edge_kernel(blocks, ids_ref, front_ref, *refs):
    out_refs, (buf, sem) = refs[:-2], refs[-2:]
    chunk, col_size = front_ref.shape[2], front_ref.shape[4]
    copies = [
        pltpu.make_async_copy(
            front_ref.at[a, 0, :, b, :, pl.ds(half * LANES, LANES)], buf.at[i, half], sem.at[i, half]
        )
        for i, (a, b) in enumerate(blocks)
        for half in range(2)
    ]
    for copy in copies:
        copy.start()
    for copy in copies:
        copy.wait()
    for i in range(len(blocks)):
        for half in range(2):
            flat = buf.at[i, half].reshape(chunk * col_size, LANES)
            for k, out_ref in enumerate(out_refs):
                out_ref[i, :, half * LANES : (half + 1) * LANES] = flat[
                    pl.ds(lax.bitwise_xor(ids_ref[1], k), chunk, stride=col_size), :
                ]


def pack_edge(ids, front, blocks):
    chunk, col_size, width = front.shape[2], front.shape[4], front.shape[5]
    vmem = pl.BlockSpec(memory_space=pltpu.VMEM)
    return pl.pallas_call(
        functools.partial(edge_kernel, blocks),
        out_shape=[jax.ShapeDtypeStruct((len(blocks), chunk, width), jnp.float32)] * col_size,
        in_specs=[pl.BlockSpec(memory_space=pltpu.SMEM), pl.BlockSpec(memory_space=pltpu.HBM)],
        out_specs=[vmem] * col_size,
        scratch_shapes=[
            pltpu.VMEM((len(blocks), 2, chunk, col_size, LANES), jnp.float32),
            pltpu.SemaphoreType.DMA((len(blocks), 2)),
        ],
        compiler_params=pltpu.CompilerParams(vmem_limit_bytes=VMEM_LIMIT),
        name="pack_edge",
    )(ids, front)


def finish_kernel(
    depths,
    shared,
    edges,
    row_size,
    col_size,
    ids_ref,
    own_ref,
    recv_ref,
    rows_ref,
    high_ref,
    low_ref,
    kids_ref,
    *rest,
):
    edge_refs = rest[:col_size]
    out_ref, in_buf, row_buf, out_buf, high_buf, low_buf, kid_buf, *sems = rest[-13:]
    in_sem, row_sem, out_sem, col_sem, kid_sem, edge_sem = sems
    my_row, my_col = ids_ref[0], ids_ref[1]
    width = high_ref.shape[1]
    chunk = width // col_size
    halves = width // LANES
    blocks = high_ref.shape[0]
    stride = blocks * halves

    counts = [n + (edge is not None) for n, edge in zip(shared, edges)]

    def fetch(i):
        a, nb, edge, slot, first = depths[i], shared[i], edges[i], i % 2, sum(shared[:i])
        copies = [pltpu.make_async_copy(rows_ref.at[a], row_buf.at[slot], row_sem.at[slot])]
        if nb:
            copies.append(
                pltpu.make_async_copy(
                    recv_ref.at[:, pl.ds(first, nb)],
                    in_buf.at[slot, :, pl.ds(0, nb)],
                    in_sem.at[slot],
                )
            )
        if edge is not None:
            for k, edge_ref in enumerate(edge_refs):
                copies.append(
                    pltpu.make_async_copy(
                        edge_ref.at[edge],
                        in_buf.at[slot, lax.bitwise_xor(my_col, k), nb],
                        edge_sem.at[slot, k],
                    )
                )
        return copies

    def send(i):
        return pltpu.make_async_copy(out_buf.at[i % 2], out_ref.at[depths[i]], out_sem.at[i % 2])

    most = high_buf.shape[0]
    columns = [
        pltpu.make_async_copy(high_ref.at[pl.ds(0, most)], high_buf, col_sem.at[0]),
        pltpu.make_async_copy(low_ref.at[pl.ds(0, most)], low_buf, col_sem.at[1]),
    ]
    steps = len(depths)
    for copy in (*fetch(0), *columns):
        copy.start()
    for i in range(steps):
        a, nb, slot = depths[i], counts[i], i % 2
        if i + 1 < steps:
            for copy in fetch(i + 1):
                copy.start()
        for copy in fetch(i):
            copy.wait()
        if i == 0:
            for copy in columns:
                copy.wait()
        if i >= 2:
            send(i - 2).wait()
        for n in range(kids_ref.shape[0]):

            @pl.when(own_ref[0, n] == a)
            def _():
                copy = pltpu.make_async_copy(kids_ref.at[n], kid_buf, kid_sem)
                copy.start()
                copy.wait()
                in_buf[slot, :, own_ref[1, n]] += kid_buf[...].reshape(col_size, chunk, width)

        tile_i = a * row_size + my_row

        def store(b, tile):
            for half in range(halves):
                out_buf[slot, pl.ds(b * halves + half, width, stride=stride), :] = tile[
                    :, half * LANES : (half + 1) * LANES
                ]

        row_high, row_low = halves_of(row_buf[slot])

        def update(b):
            return bf16_nt(row_high, high_buf[b]) + (
                bf16_nt(row_high, low_buf[b]) + bf16_nt(row_low, high_buf[b])
            )

        for b in range(nb):
            tile = in_buf[slot, :, b].reshape(width, width)
            tile_j = b * col_size + my_col
            if b < nb - 1:
                store(b, tile - update(b))
            else:

                @pl.when(tile_i > tile_j)
                def _():
                    store(b, tile - update(b))

                @pl.when(tile_i == tile_j)
                def _():
                    store(b, 0.5 * (tile + tile.T) - update(b))

                @pl.when(tile_i < tile_j)
                def _():
                    store(b, jnp.zeros_like(tile))

        @pl.when(my_col == 0)
        def _():
            store(0, row_buf[slot])

        zero = jnp.zeros((width, LANES), jnp.float32)
        filled = counts[i - 2] * halves if i >= 2 else stride
        for n in range(nb * halves, filled):
            out_buf[slot, pl.ds(n, width, stride=stride), :] = zero
        send(i).start()
    for i in range(max(steps - 2, 0), steps):
        send(i).wait()


def finish(
    depths, shared, edges, row_size, col_size, ids, own, recv, rows, high, low, kids, edge, out=None
):
    smem = pl.BlockSpec(memory_space=pltpu.SMEM)
    hbm = pl.BlockSpec(memory_space=pltpu.HBM)
    blocks, width = high.shape[0], high.shape[1]
    chunk = width // col_size
    lines = width * blocks * (width // LANES)
    counts = [n + (edge is not None) for n, edge in zip(shared, edges)]
    operands = [ids, own, recv, rows, high, low, kids, *edge]
    in_specs = [smem, smem] + [hbm] * (5 + len(edge))
    aliases = {}
    if out is not None:
        operands.append(out)
        in_specs.append(hbm)
        aliases = {len(operands) - 1: 0}
    return pl.pallas_call(
        functools.partial(finish_kernel, depths, shared, edges, row_size, col_size),
        out_shape=jax.ShapeDtypeStruct((rows.shape[0], lines, LANES), jnp.float32),
        in_specs=in_specs,
        out_specs=hbm,
        scratch_shapes=[
            pltpu.VMEM((2, col_size, max(counts), chunk, width), jnp.float32),
            pltpu.VMEM((2, width, width), jnp.float32),
            pltpu.VMEM((2, lines, LANES), jnp.float32),
            pltpu.VMEM((max(counts), width, width), jnp.bfloat16),
            pltpu.VMEM((max(counts), width, width), jnp.bfloat16),
            pltpu.VMEM((width, width), jnp.float32),
            pltpu.SemaphoreType.DMA((2,)),
            pltpu.SemaphoreType.DMA((2,)),
            pltpu.SemaphoreType.DMA((2,)),
            pltpu.SemaphoreType.DMA((2,)),
            pltpu.SemaphoreType.DMA,
            pltpu.SemaphoreType.DMA((2, col_size)),
        ],
        input_output_aliases=aliases,
        compiler_params=pltpu.CompilerParams(vmem_limit_bytes=VMEM_LIMIT),
        name="finish",
    )(*operands)


def factor_and_inverse(corner):
    size = corner.shape[0] // 2
    eye = jnp.eye(size, dtype=jnp.float32)

    def both(block):
        factor = lax.linalg.cholesky(block, symmetrize_input=False)
        return factor, jax.scipy.linalg.solve_triangular(factor, eye, lower=True)

    def product(left, right):
        return jnp.dot(left, right, precision=HIGHEST)

    top, top_inverse = both(corner[:size, :size])
    below = product(corner[size:, :size], top_inverse.T)
    end, end_inverse = both(corner[size:, size:] - product(below, below.T))
    corner_inverse = -product(end_inverse, product(below, top_inverse))
    zero = jnp.zeros_like(eye)
    return (
        jnp.block([[top, zero], [below, end]]),
        jnp.block([[top_inverse, zero], [corner_inverse, end_inverse]]),
    )


def on_device(front, child_tiles, child_rows, child_cols, child_counts, row_maps, col_maps):
    row_size, col_size = lax.axis_size("row"), lax.axis_size("col")
    my_row, my_col = lax.axis_index("row"), lax.axis_index("col")
    row_tiles, chunk, col_tiles, width = front.shape[0], front.shape[2], front.shape[3], front.shape[5]
    slots = child_tiles.shape[2]
    capacity = slots // 4
    arrivals = row_size * capacity
    group = col_size // row_size
    ids = jnp.stack([my_row, my_col]).astype(jnp.int32)

    shared = [shared_blocks(a, row_size, col_size) for a in range(row_tiles)]
    edge_blocks = [
        (a, shared[a]) for a in range(row_tiles) if depth_blocks(a, row_size, col_size) > shared[a]
    ]
    edge_of = {a: i for i, (a, _) in enumerate(edge_blocks)}
    rest = [a for a in range(row_tiles - 1, -1, -1) if a != row_tiles - 2]
    total = sum(shared[a] for a in rest)
    deep = next(n for n in range(len(rest)) if 9 * sum(shared[a] for a in rest[:n]) >= 4 * total)
    parts = [[row_tiles - 2], rest[deep:], rest[:deep]]

    def packed(part, *after):
        held = lax.optimization_barrier((front,) + after)[0]
        sent = [a for a in part if shared[a]]
        return pack(held, sent, [shared[a] for a in sent])

    def exchange(blocks, *after):
        blocks = lax.optimization_barrier((blocks,) + after)[0]
        return lax.all_to_all(blocks, "col", split_axis=0, concat_axis=0, tiled=True)

    def along_row(shift):
        return [(r, (r + shift) % row_size) for r in range(row_size)]

    def across_col(k):
        return [(c, c ^ k) for c in range(col_size)]

    moved = move_tiles(
        row_size,
        col_size,
        capacity,
        ids,
        child_rows.reshape(slots),
        child_cols.reshape(slots),
        child_counts.reshape(1),
        child_tiles.reshape(slots, width, width),
        row_maps.reshape(slots, width),
        col_maps.reshape(slots, width),
    )
    moved, pieces = moved[:row_size], moved[row_size:]

    sent = [
        lax.ppermute(pieces[pair], "col", [(0, 2 * pair)]) for pair in range(1, col_size // 2)
    ]
    edge = pack_edge(ids, lax.optimization_barrier((front, pieces[0]))[0], edge_blocks)

    def send_edge(k, value):
        steps = [
            (r * col_size + c, r * col_size + (c ^ k))
            for r in range(row_size)
            for c in range(col_size)
            if c ^ k <= r
        ]
        return lax.ppermute(value, ("row", "col"), steps)

    half = col_size // 2
    far = [send_edge(k, edge[k]) for k in range(half, col_size)]
    second = packed(parts[1], pieces[0])
    blocks = packed(parts[0], pieces[0])
    first = first_rows(front)
    *sent, blocks, _ = lax.optimization_barrier((*sent, blocks, *far[:1]))
    arrived = [exchange(blocks, *sent, *far)]
    lead = jnp.where(my_col == 0, pieces[0], sum(sent[1:], sent[0]))
    other = lax.ppermute(lead[1], "col", [(c, c + 1) for c in range(0, col_size, 2)])
    other, second, first = lax.optimization_barrier((other, second, first))
    lead = jnp.where(my_col % 2 == 0, lead[0], other)
    lead = [lead[0]] + [
        lax.ppermute(lead[shift], "row", along_row(shift)) for shift in range(1, row_size)
    ]
    raw = lead_rows(capacity, first, lead)

    steps = range(2, half, 2)
    across = lax.ppermute(raw, "col", across_col(half))
    inner = [lax.ppermute(raw, "col", across_col(k)) for k in steps]
    near = [send_edge(k, lax.optimization_barrier((edge[k], raw))[0]) for k in range(1, half)]
    arrived.append(exchange(second, arrived[0], across, *inner, *near))
    outer = [lax.ppermute(across, "col", across_col(k)) for k in steps]
    known = [raw, *inner, across]
    third = packed(parts[2], across)
    stacked, third = lax.optimization_barrier((jnp.stack(known), third))
    beside = lax.ppermute(stacked, "col", across_col(1))
    outside = lax.ppermute(jnp.stack(outer), "col", across_col(1))
    raw_rows = order_rows(ids, known + outer, jnp.concatenate([beside, outside]))
    meta = jnp.concatenate(
        [child_rows.reshape(1, slots), child_cols.reshape(1, slots), child_counts.reshape(1, 1)], axis=1
    )
    meta, _ = lax.optimization_barrier((meta, across))
    meta = lax.all_gather(meta, "row", axis=0, tiled=True)
    own = locate(row_size, capacity, slots, ids, meta)
    *moved, _ = lax.optimization_barrier((*moved, across))
    kids = jnp.concatenate(
        [moved[0]]
        + [lax.ppermute(moved[shift], "row", along_row(shift)) for shift in range(1, row_size)]
    )

    arrived.append(exchange(third, arrived[1], beside, outside, own, kids))
    edge = [edge[0], *near, *far]

    corner_mine = corner = raw_rows[:, 0].reshape(width, width)
    corner = jnp.where(my_row == 0, corner, 0.0)
    for shift in range(1, row_size):
        corner = corner + lax.ppermute(corner_mine, "row", [(0, shift)])
    corner = 0.5 * (corner + corner.T)
    factor, inverse = factor_and_inverse(corner)

    mine = lax.dynamic_index_in_dim(
        raw_rows.reshape(col_size, col_tiles, group, chunk, width),
        my_col // row_size,
        2,
        keepdims=False,
    )
    raw_cols = jnp.where(my_row == my_col % row_size, mine, 0.0)
    for shift in range(1, row_size):
        steps = [
            ((c % row_size) * col_size + c, ((c + shift) % row_size) * col_size + c)
            for c in range(col_size)
        ]
        raw_cols = raw_cols + lax.ppermute(mine, ("row", "col"), steps)
    rows, high, low = panels(ids, inverse, factor, raw_rows, raw_cols)

    out = None
    for step, part in enumerate(parts):
        out = finish(
            part,
            [shared[a] for a in part],
            [edge_of.get(a) for a in part],
            row_size,
            col_size,
            ids,
            own,
            arrived[step],
            rows,
            high,
            low,
            kids,
            edge,
            out,
        )
    return out.reshape(row_tiles, 1, width, col_tiles, 1, width)


def solution(mesh):
    return jax.shard_map(
        on_device,
        mesh=mesh,
        in_specs=(
            P(None, "row", "col", None, None, None),
            P("row", "col", None, None, None),
            P("row", "col", None),
            P("row", "col", None),
            P("row", "col"),
            P("row", "col", None, None),
            P("row", "col", None, None),
        ),
        out_specs=P(None, "row", None, None, "col", None),
        check_vma=False,
    )
```

```python
import functools

import jax
import jax.numpy as jnp
from jax import lax
from jax.experimental import pallas as pl
from jax.experimental.pallas import tpu as pltpu
from jax.sharding import PartitionSpec as P

HIGHEST = lax.Precision.HIGHEST
LANES = 128
VMEM_LIMIT = 60 << 20


def bf16_nt(left, right):
    return lax.dot_general(
        left, right, (((1,), (1,)), ((), ())), preferred_element_type=jnp.float32
    )


def depth_blocks(a, row_size, col_size):
    return (a * row_size + row_size - 1) // col_size + 1


def shared_blocks(a, row_size, col_size):
    return (a * row_size + row_size - 1 - col_size // 2) // col_size + 1


def move_kernel(
    row_size,
    capacity,
    ids_ref,
    rows_ref,
    cols_ref,
    count_ref,
    tiles_ref,
    row_map_ref,
    col_map_ref,
    *out_refs,
):
    slots, width = tiles_ref.shape[0], tiles_ref.shape[1]
    out_refs, lead_refs = out_refs[:row_size], out_refs[row_size:]
    chunk = width // (2 * len(lead_refs))
    labels = lax.broadcasted_iota(jnp.int32, (width, width), 0)
    count = count_ref[0]

    def one(shift, place, out_ref):
        owner = lax.rem(ids_ref[0] + shift, row_size)
        def scan(k, state):
            chosen, seen = state
            hit = (lax.rem(rows_ref[k], row_size) == owner) & (k < count)
            chosen = jnp.where(hit & (seen == place), k, chosen)
            return chosen, seen + hit.astype(jnp.int32)

        chosen, seen = lax.fori_loop(0, slots, scan, (jnp.int32(0), jnp.int32(0)))
        row_hot = (labels == row_map_ref[pl.ds(chosen, 1), :]).astype(jnp.bfloat16)
        col_hot = (labels == col_map_ref[pl.ds(chosen, 1), :]).astype(jnp.bfloat16)
        left = tiles_ref[chosen]
        tile = None
        for _ in range(3):
            term = left.astype(jnp.bfloat16)
            left = left - term.astype(jnp.float32)
            moved = jnp.dot(row_hot, term, preferred_element_type=jnp.float32)
            moved = bf16_nt(moved.astype(jnp.bfloat16), col_hot)
            tile = moved if tile is None else tile + moved
        out_ref[place] = tile
        here = (seen > place) & (cols_ref[chosen] == 0)
        target = jnp.where(here, rows_ref[chosen] // row_size, -1).astype(jnp.float32)
        mark = jnp.full((1, width), target)
        for pair, lead_ref in enumerate(lead_refs):
            for side in range(2):
                first = (2 * pair + side) * chunk
                lead_ref[side, shift, pl.ds(place * chunk, chunk), :] = tile[first : first + chunk]
                lead_ref[side, shift, pl.ds(capacity * chunk + place, 1), :] = mark

    for shift, out_ref in enumerate(out_refs):
        for place in range(capacity):
            one(shift, place, out_ref)


def move_tiles(row_size, col_size, capacity, ids, rows, cols, count, tiles, row_maps, col_maps):
    slots, width = tiles.shape[0], tiles.shape[1]
    smem = pl.BlockSpec(memory_space=pltpu.SMEM)
    vmem = pl.BlockSpec(memory_space=pltpu.VMEM)
    return pl.pallas_call(
        functools.partial(move_kernel, row_size, capacity),
        out_shape=[jax.ShapeDtypeStruct((capacity, width, width), jnp.float32)] * row_size
        + [
            jax.ShapeDtypeStruct(
                (2, row_size, capacity * (width // col_size) + 8, width), jnp.float32
            )
        ]
        * (col_size // 2),
        in_specs=[smem, smem, smem, smem, vmem, vmem, vmem],
        out_specs=[vmem] * (row_size + col_size // 2),
        compiler_params=pltpu.CompilerParams(vmem_limit_bytes=VMEM_LIMIT),
        name="move_tiles",
    )(ids, rows, cols, count, tiles, row_maps, col_maps)


def locate_kernel(row_size, capacity, slots, ids_ref, meta_ref, own_ref):
    my_row = ids_ref[0]

    def clear(n, carry):
        own_ref[0, n] = -1
        own_ref[1, n] = -1
        return carry

    lax.fori_loop(0, row_size * capacity, clear, 0)

    def source(s, carry):
        line = lax.rem(my_row + row_size - s, row_size)
        count = meta_ref[line, 2 * slots]

        def slot(k, seen):
            target = meta_ref[line, k]
            hit = (lax.rem(target, row_size) == my_row) & (k < count)

            @pl.when(hit)
            def _():
                own_ref[0, s * capacity + seen] = target // row_size
                own_ref[1, s * capacity + seen] = meta_ref[line, slots + k]

            return jnp.minimum(seen + hit.astype(jnp.int32), capacity - 1)

        lax.fori_loop(0, slots, slot, jnp.int32(0))
        return carry

    lax.fori_loop(0, row_size, source, 0)


def locate(row_size, capacity, slots, ids, meta):
    smem = pl.BlockSpec(memory_space=pltpu.SMEM)
    return pl.pallas_call(
        functools.partial(locate_kernel, row_size, capacity, slots),
        out_shape=jax.ShapeDtypeStruct((2, row_size * capacity), jnp.int32),
        in_specs=[smem, smem],
        out_specs=smem,
        name="locate",
    )(ids, meta)


def first_kernel(front_ref, out_ref, buf, sem):
    row_tiles, chunk, col_size = front_ref.shape[0], front_ref.shape[2], front_ref.shape[4]
    copies = [
        pltpu.make_async_copy(
            front_ref.at[:, 0, :, 0, :, pl.ds(half * LANES, LANES)], buf.at[half], sem.at[half]
        )
        for half in range(2)
    ]
    for copy in copies:
        copy.start()
    for copy in copies:
        copy.wait()
    for half in range(2):
        flat = buf.at[half].reshape(row_tiles * chunk * col_size, LANES)
        for a in range(row_tiles):
            out_ref[a, :, half * LANES : (half + 1) * LANES] = flat[
                pl.ds(a * chunk * col_size, chunk, stride=col_size), :
            ]


def first_rows(front):
    row_tiles, chunk, col_size, width = front.shape[0], front.shape[2], front.shape[4], front.shape[5]
    return pl.pallas_call(
        first_kernel,
        out_shape=jax.ShapeDtypeStruct((row_tiles, chunk, width), jnp.float32),
        in_specs=[pl.BlockSpec(memory_space=pltpu.HBM)],
        out_specs=pl.BlockSpec(memory_space=pltpu.VMEM),
        scratch_shapes=[
            pltpu.VMEM((2, row_tiles, chunk, col_size, LANES), jnp.float32),
            pltpu.SemaphoreType.DMA((2,)),
        ],
        compiler_params=pltpu.CompilerParams(vmem_limit_bytes=VMEM_LIMIT),
        name="first_rows",
    )(front)


def lead_kernel(capacity, own_ref, *refs):
    kids_refs, out_ref = refs[:-1], refs[-1]
    chunk = own_ref.shape[1]

    def one(a, carry):
        total = own_ref[a]
        for kids_ref in kids_refs:
            for place in range(capacity):
                kid = kids_ref[pl.ds(place * chunk, chunk), :]
                target = kids_ref[pl.ds(capacity * chunk + place, 1), :]
                total += jnp.where(target == a.astype(jnp.float32), kid, 0.0)
        out_ref[a] = total
        return carry

    lax.fori_loop(0, own_ref.shape[0], one, 0)


def lead_rows(capacity, own, kids):
    vmem = pl.BlockSpec(memory_space=pltpu.VMEM)
    return pl.pallas_call(
        functools.partial(lead_kernel, capacity),
        out_shape=jax.ShapeDtypeStruct(own.shape, jnp.float32),
        in_specs=[vmem] * (1 + len(kids)),
        out_specs=vmem,
        compiler_params=pltpu.CompilerParams(vmem_limit_bytes=VMEM_LIMIT),
        name="lead_rows",
    )(own, *kids)


def order_kernel(ids_ref, *refs):
    same, other_ref, out_ref = refs[:-2], refs[-2], refs[-1]
    for k, same_ref in enumerate(same):
        out_ref[lax.bitwise_xor(ids_ref[1], 2 * k)] = same_ref[...]
        out_ref[lax.bitwise_xor(ids_ref[1], 2 * k + 1)] = other_ref[k]


def order_rows(ids, same, other):
    smem = pl.BlockSpec(memory_space=pltpu.SMEM)
    vmem = pl.BlockSpec(memory_space=pltpu.VMEM)
    return pl.pallas_call(
        order_kernel,
        out_shape=jax.ShapeDtypeStruct((2 * len(same),) + same[0].shape, jnp.float32),
        in_specs=[smem] + [vmem] * (1 + len(same)),
        out_specs=vmem,
        compiler_params=pltpu.CompilerParams(vmem_limit_bytes=VMEM_LIMIT),
        name="order_rows",
    )(ids, *same, other)


def halves_of(value):
    high = value.astype(jnp.bfloat16)
    return high, (value - high.astype(jnp.float32)).astype(jnp.bfloat16)


def panel_kernel(ids_ref, inverse_ref, factor_ref, rows_ref, cols_ref, row_out, high_out, low_out):
    width = inverse_ref.shape[0]
    high, low = halves_of(inverse_ref[...])

    def solve(tile):
        tile_high, tile_low = halves_of(tile)
        return bf16_nt(tile_high, high) + (bf16_nt(tile_high, low) + bf16_nt(tile_low, high))

    def row(a, carry):
        row_out[a] = solve(rows_ref[:, a].reshape(width, width))
        return carry

    lax.fori_loop(0, row_out.shape[0], row, 0)

    @pl.when(ids_ref[0] == 0)
    def _():
        row_out[0] = factor_ref[...]

    def column(b, carry):
        col = solve(cols_ref[:, b].reshape(width, width))
        high_out[b], low_out[b] = halves_of(col)
        return carry

    lax.fori_loop(0, high_out.shape[0], column, 0)


def panels(ids, inverse, factor, rows, cols):
    smem = pl.BlockSpec(memory_space=pltpu.SMEM)
    vmem = pl.BlockSpec(memory_space=pltpu.VMEM)
    width = inverse.shape[0]
    return pl.pallas_call(
        panel_kernel,
        out_shape=(
            jax.ShapeDtypeStruct((rows.shape[1], width, width), jnp.float32),
            jax.ShapeDtypeStruct((cols.shape[1], width, width), jnp.bfloat16),
            jax.ShapeDtypeStruct((cols.shape[1], width, width), jnp.bfloat16),
        ),
        in_specs=[smem, vmem, vmem, vmem, vmem],
        out_specs=(vmem, vmem, vmem),
        compiler_params=pltpu.CompilerParams(vmem_limit_bytes=VMEM_LIMIT),
        name="panels",
    )(ids, inverse, factor, rows, cols)


def pack_kernel(depths, counts, front_ref, out_ref, in_buf, out_buf, in_sem, out_sem):
    col_size = front_ref.shape[4]
    chunk = front_ref.shape[2]

    def fetch(i):
        a, nb, slot = depths[i], counts[i], i % 2
        return [
            pltpu.make_async_copy(
                front_ref.at[a, 0, :, pl.ds(0, nb), :, pl.ds(half * LANES, LANES)],
                in_buf.at[slot, half, :, pl.ds(0, nb)],
                in_sem.at[slot, half],
            )
            for half in range(2)
        ]

    def send(i):
        first, nb, slot = sum(counts[:i]), counts[i], i % 2
        return pltpu.make_async_copy(
            out_buf.at[slot, :, pl.ds(0, nb)], out_ref.at[:, pl.ds(first, nb)], out_sem.at[slot]
        )

    steps = len(depths)
    for copy in fetch(0):
        copy.start()
    for i in range(steps):
        slot, nb = i % 2, counts[i]
        if i + 1 < steps:
            for copy in fetch(i + 1):
                copy.start()
        for copy in fetch(i):
            copy.wait()
        if i >= 2:
            send(i - 2).wait()
        for half in range(2):
            total = in_buf.shape[3]
            flat = in_buf.at[slot, half].reshape(chunk * total * col_size, LANES)
            for b in range(nb):
                for c in range(col_size):
                    out_buf[slot, c, b, :, half * LANES : (half + 1) * LANES] = flat[
                        pl.ds(b * col_size + c, chunk, stride=total * col_size), :
                    ]
        send(i).start()
    for i in range(max(steps - 2, 0), steps):
        send(i).wait()


def pack(front, depths, counts):
    chunk, col_size, width = front.shape[2], front.shape[4], front.shape[5]
    most = max(counts)
    return pl.pallas_call(
        functools.partial(pack_kernel, depths, counts),
        out_shape=jax.ShapeDtypeStruct((col_size, sum(counts), chunk, width), jnp.float32),
        in_specs=[pl.BlockSpec(memory_space=pltpu.HBM)],
        out_specs=pl.BlockSpec(memory_space=pltpu.HBM),
        scratch_shapes=[
            pltpu.VMEM((2, 2, chunk, most, col_size, LANES), jnp.float32),
            pltpu.VMEM((2, col_size, most, chunk, width), jnp.float32),
            pltpu.SemaphoreType.DMA((2, 2)),
            pltpu.SemaphoreType.DMA((2,)),
        ],
        compiler_params=pltpu.CompilerParams(vmem_limit_bytes=VMEM_LIMIT),
        name="pack",
    )(front)


def edge_kernel(blocks, ids_ref, front_ref, *refs):
    out_refs, (buf, sem) = refs[:-2], refs[-2:]
    chunk, col_size = front_ref.shape[2], front_ref.shape[4]
    copies = [
        pltpu.make_async_copy(
            front_ref.at[a, 0, :, b, :, pl.ds(half * LANES, LANES)], buf.at[i, half], sem.at[i, half]
        )
        for i, (a, b) in enumerate(blocks)
        for half in range(2)
    ]
    for copy in copies:
        copy.start()
    for copy in copies:
        copy.wait()
    for i in range(len(blocks)):
        for half in range(2):
            flat = buf.at[i, half].reshape(chunk * col_size, LANES)
            for k, out_ref in enumerate(out_refs):
                out_ref[i, :, half * LANES : (half + 1) * LANES] = flat[
                    pl.ds(lax.bitwise_xor(ids_ref[1], k), chunk, stride=col_size), :
                ]


def pack_edge(ids, front, blocks):
    chunk, col_size, width = front.shape[2], front.shape[4], front.shape[5]
    vmem = pl.BlockSpec(memory_space=pltpu.VMEM)
    return pl.pallas_call(
        functools.partial(edge_kernel, blocks),
        out_shape=[jax.ShapeDtypeStruct((len(blocks), chunk, width), jnp.float32)] * col_size,
        in_specs=[pl.BlockSpec(memory_space=pltpu.SMEM), pl.BlockSpec(memory_space=pltpu.HBM)],
        out_specs=[vmem] * col_size,
        scratch_shapes=[
            pltpu.VMEM((len(blocks), 2, chunk, col_size, LANES), jnp.float32),
            pltpu.SemaphoreType.DMA((len(blocks), 2)),
        ],
        compiler_params=pltpu.CompilerParams(vmem_limit_bytes=VMEM_LIMIT),
        name="pack_edge",
    )(ids, front)


def finish_kernel(
    depths,
    shared,
    edges,
    row_size,
    col_size,
    ids_ref,
    own_ref,
    recv_ref,
    rows_ref,
    high_ref,
    low_ref,
    kids_ref,
    *rest,
):
    edge_refs = rest[:col_size]
    out_ref, in_buf, row_buf, out_buf, high_buf, low_buf, kid_buf, *sems = rest[-13:]
    in_sem, row_sem, out_sem, col_sem, kid_sem, edge_sem = sems
    my_row, my_col = ids_ref[0], ids_ref[1]
    width = high_ref.shape[1]
    chunk = width // col_size
    halves = width // LANES
    blocks = high_ref.shape[0]
    stride = blocks * halves

    counts = [n + (edge is not None) for n, edge in zip(shared, edges)]

    def fetch(i):
        a, nb, edge, slot, first = depths[i], shared[i], edges[i], i % 2, sum(shared[:i])
        copies = [pltpu.make_async_copy(rows_ref.at[a], row_buf.at[slot], row_sem.at[slot])]
        if nb:
            copies.append(
                pltpu.make_async_copy(
                    recv_ref.at[:, pl.ds(first, nb)],
                    in_buf.at[slot, :, pl.ds(0, nb)],
                    in_sem.at[slot],
                )
            )
        if edge is not None:
            for k, edge_ref in enumerate(edge_refs):
                copies.append(
                    pltpu.make_async_copy(
                        edge_ref.at[edge],
                        in_buf.at[slot, lax.bitwise_xor(my_col, k), nb],
                        edge_sem.at[slot, k],
                    )
                )
        return copies

    def send(i):
        return pltpu.make_async_copy(out_buf.at[i % 2], out_ref.at[depths[i]], out_sem.at[i % 2])

    most = high_buf.shape[0]
    columns = [
        pltpu.make_async_copy(high_ref.at[pl.ds(0, most)], high_buf, col_sem.at[0]),
        pltpu.make_async_copy(low_ref.at[pl.ds(0, most)], low_buf, col_sem.at[1]),
    ]
    steps = len(depths)
    for copy in (*fetch(0), *columns):
        copy.start()
    for i in range(steps):
        a, nb, slot = depths[i], counts[i], i % 2
        if i + 1 < steps:
            for copy in fetch(i + 1):
                copy.start()
        for copy in fetch(i):
            copy.wait()
        if i == 0:
            for copy in columns:
                copy.wait()
        if i >= 2:
            send(i - 2).wait()
        for n in range(kids_ref.shape[0]):

            @pl.when(own_ref[0, n] == a)
            def _():
                copy = pltpu.make_async_copy(kids_ref.at[n], kid_buf, kid_sem)
                copy.start()
                copy.wait()
                in_buf[slot, :, own_ref[1, n]] += kid_buf[...].reshape(col_size, chunk, width)

        tile_i = a * row_size + my_row

        def store(b, tile):
            for half in range(halves):
                out_buf[slot, pl.ds(b * halves + half, width, stride=stride), :] = tile[
                    :, half * LANES : (half + 1) * LANES
                ]

        row_high, row_low = halves_of(row_buf[slot])

        def update(b):
            return bf16_nt(row_high, high_buf[b]) + (
                bf16_nt(row_high, low_buf[b]) + bf16_nt(row_low, high_buf[b])
            )

        for b in range(nb):
            tile = in_buf[slot, :, b].reshape(width, width)
            tile_j = b * col_size + my_col
            if b < nb - 1:
                store(b, tile - update(b))
            else:

                @pl.when(tile_i > tile_j)
                def _():
                    store(b, tile - update(b))

                @pl.when(tile_i == tile_j)
                def _():
                    store(b, 0.5 * (tile + tile.T) - update(b))

                @pl.when(tile_i < tile_j)
                def _():
                    store(b, jnp.zeros_like(tile))

        @pl.when(my_col == 0)
        def _():
            store(0, row_buf[slot])

        zero = jnp.zeros((width, LANES), jnp.float32)
        for n in range(nb * halves, stride):
            out_buf[slot, pl.ds(n, width, stride=stride), :] = zero
        send(i).start()
    for i in range(max(steps - 2, 0), steps):
        send(i).wait()


def finish(
    depths, shared, edges, row_size, col_size, ids, own, recv, rows, high, low, kids, edge, out=None
):
    smem = pl.BlockSpec(memory_space=pltpu.SMEM)
    hbm = pl.BlockSpec(memory_space=pltpu.HBM)
    blocks, width = high.shape[0], high.shape[1]
    chunk = width // col_size
    lines = width * blocks * (width // LANES)
    counts = [n + (edge is not None) for n, edge in zip(shared, edges)]
    operands = [ids, own, recv, rows, high, low, kids, *edge]
    in_specs = [smem, smem] + [hbm] * (5 + len(edge))
    aliases = {}
    if out is not None:
        operands.append(out)
        in_specs.append(hbm)
        aliases = {len(operands) - 1: 0}
    return pl.pallas_call(
        functools.partial(finish_kernel, depths, shared, edges, row_size, col_size),
        out_shape=jax.ShapeDtypeStruct((rows.shape[0], lines, LANES), jnp.float32),
        in_specs=in_specs,
        out_specs=hbm,
        scratch_shapes=[
            pltpu.VMEM((2, col_size, max(counts), chunk, width), jnp.float32),
            pltpu.VMEM((2, width, width), jnp.float32),
            pltpu.VMEM((2, lines, LANES), jnp.float32),
            pltpu.VMEM((max(counts), width, width), jnp.bfloat16),
            pltpu.VMEM((max(counts), width, width), jnp.bfloat16),
            pltpu.VMEM((width, width), jnp.float32),
            pltpu.SemaphoreType.DMA((2,)),
            pltpu.SemaphoreType.DMA((2,)),
            pltpu.SemaphoreType.DMA((2,)),
            pltpu.SemaphoreType.DMA((2,)),
            pltpu.SemaphoreType.DMA,
            pltpu.SemaphoreType.DMA((2, col_size)),
        ],
        input_output_aliases=aliases,
        compiler_params=pltpu.CompilerParams(vmem_limit_bytes=VMEM_LIMIT),
        name="finish",
    )(*operands)


def factor_and_inverse(corner):
    size = corner.shape[0] // 2
    eye = jnp.eye(size, dtype=jnp.float32)

    def both(block):
        factor = lax.linalg.cholesky(block, symmetrize_input=False)
        return factor, jax.scipy.linalg.solve_triangular(factor, eye, lower=True)

    def product(left, right):
        return jnp.dot(left, right, precision=HIGHEST)

    top, top_inverse = both(corner[:size, :size])
    below = product(corner[size:, :size], top_inverse.T)
    end, end_inverse = both(corner[size:, size:] - product(below, below.T))
    corner_inverse = -product(end_inverse, product(below, top_inverse))
    zero = jnp.zeros_like(eye)
    return (
        jnp.block([[top, zero], [below, end]]),
        jnp.block([[top_inverse, zero], [corner_inverse, end_inverse]]),
    )


def on_device(front, child_tiles, child_rows, child_cols, child_counts, row_maps, col_maps):
    row_size, col_size = lax.axis_size("row"), lax.axis_size("col")
    my_row, my_col = lax.axis_index("row"), lax.axis_index("col")
    row_tiles, chunk, col_tiles, width = front.shape[0], front.shape[2], front.shape[3], front.shape[5]
    slots = child_tiles.shape[2]
    capacity = slots // 4
    arrivals = row_size * capacity
    group = col_size // row_size
    ids = jnp.stack([my_row, my_col]).astype(jnp.int32)

    shared = [shared_blocks(a, row_size, col_size) for a in range(row_tiles)]
    edge_blocks = [
        (a, shared[a]) for a in range(row_tiles) if depth_blocks(a, row_size, col_size) > shared[a]
    ]
    edge_of = {a: i for i, (a, _) in enumerate(edge_blocks)}
    last = (row_tiles - 5) * 3 // 4 + 1
    parts = [[row_tiles - 2], [row_tiles - 1, row_tiles - 3, row_tiles - 4]]
    parts.append([a for a in range(row_tiles - 5, -1, -1) if a != last])
    parts.append([last])

    def packed(part, *after):
        held = lax.optimization_barrier((front,) + after)[0]
        sent = [a for a in part if shared[a]]
        return pack(held, sent, [shared[a] for a in sent])

    def exchange(blocks, *after):
        blocks = lax.optimization_barrier((blocks,) + after)[0]
        return lax.all_to_all(blocks, "col", split_axis=0, concat_axis=0, tiled=True)

    def along_row(shift):
        return [(r, (r + shift) % row_size) for r in range(row_size)]

    def across_col(k):
        return [(c, c ^ k) for c in range(col_size)]

    moved = move_tiles(
        row_size,
        col_size,
        capacity,
        ids,
        child_rows.reshape(slots),
        child_cols.reshape(slots),
        child_counts.reshape(1),
        child_tiles.reshape(slots, width, width),
        row_maps.reshape(slots, width),
        col_maps.reshape(slots, width),
    )
    moved, pieces = moved[:row_size], moved[row_size:]

    sent = [
        lax.ppermute(pieces[pair], "col", [(0, 2 * pair)]) for pair in range(1, col_size // 2)
    ]
    edge = pack_edge(ids, lax.optimization_barrier((front, pieces[0]))[0], edge_blocks)

    def send_edge(k, value):
        steps = [
            (r * col_size + c, r * col_size + (c ^ k))
            for r in range(row_size)
            for c in range(col_size)
            if c ^ k <= r
        ]
        return lax.ppermute(value, ("row", "col"), steps)

    half = col_size // 2
    far = [send_edge(k, edge[k]) for k in range(half, col_size)]
    second = packed(parts[1], pieces[0])
    blocks = packed(parts[0], pieces[0])
    first = first_rows(front)
    *sent, blocks, _ = lax.optimization_barrier((*sent, blocks, *far[:1]))
    arrived = [exchange(blocks, *sent, *far)]
    lead = jnp.where(my_col == 0, pieces[0], sum(sent[1:], sent[0]))
    other = lax.ppermute(lead[1], "col", [(c, c + 1) for c in range(0, col_size, 2)])
    other, second, first = lax.optimization_barrier((other, second, first))
    lead = jnp.where(my_col % 2 == 0, lead[0], other)
    lead = [lead[0]] + [
        lax.ppermute(lead[shift], "row", along_row(shift)) for shift in range(1, row_size)
    ]
    raw = lead_rows(capacity, first, lead)

    steps = range(2, half, 2)
    across = lax.ppermute(raw, "col", across_col(half))
    inner = [lax.ppermute(raw, "col", across_col(k)) for k in steps]
    near = [send_edge(k, lax.optimization_barrier((edge[k], raw))[0]) for k in range(1, half)]
    arrived.append(exchange(second, arrived[0], across, *inner, *near))
    outer = [lax.ppermute(across, "col", across_col(k)) for k in steps]
    known = [raw, *inner, across]
    third = packed(parts[2], across)
    stacked, third = lax.optimization_barrier((jnp.stack(known), third))
    beside = lax.ppermute(stacked, "col", across_col(1))
    outside = lax.ppermute(jnp.stack(outer), "col", across_col(1))
    raw_rows = order_rows(ids, known + outer, jnp.concatenate([beside, outside]))
    meta = jnp.concatenate(
        [child_rows.reshape(1, slots), child_cols.reshape(1, slots), child_counts.reshape(1, 1)], axis=1
    )
    meta, _ = lax.optimization_barrier((meta, across))
    meta = lax.all_gather(meta, "row", axis=0, tiled=True)
    own = locate(row_size, capacity, slots, ids, meta)
    *moved, _ = lax.optimization_barrier((*moved, across))
    kids = jnp.concatenate(
        [moved[0]]
        + [lax.ppermute(moved[shift], "row", along_row(shift)) for shift in range(1, row_size)]
    )

    arrived.append(exchange(third, arrived[1], beside, outside, kids))
    edge = [edge[0], *near, *far]

    corner_mine = corner = raw_rows[:, 0].reshape(width, width)
    corner = jnp.where(my_row == 0, corner, 0.0)
    for shift in range(1, row_size):
        corner = corner + lax.ppermute(corner_mine, "row", [(0, shift)])
    corner = 0.5 * (corner + corner.T)
    factor, inverse = factor_and_inverse(corner)

    mine = lax.dynamic_index_in_dim(
        raw_rows.reshape(col_size, col_tiles, group, chunk, width),
        my_col // row_size,
        2,
        keepdims=False,
    )
    raw_cols = jnp.where(my_row == my_col % row_size, mine, 0.0)
    for shift in range(1, row_size):
        steps = [
            ((c % row_size) * col_size + c, ((c + shift) % row_size) * col_size + c)
            for c in range(col_size)
        ]
        raw_cols = raw_cols + lax.ppermute(mine, ("row", "col"), steps)
    rows, high, low = panels(ids, inverse, factor, raw_rows, raw_cols)

    out = None
    for step, part in enumerate(parts):
        if step == 2:
            arrived.append(exchange(packed(parts[3]), arrived[2], out))
        out = finish(
            part,
            [shared[a] for a in part],
            [edge_of.get(a) for a in part],
            row_size,
            col_size,
            ids,
            own,
            arrived[step],
            rows,
            high,
            low,
            kids,
            edge,
            out,
        )
    return out.reshape(row_tiles, 1, width, col_tiles, 1, width)


def solution(mesh):
    return jax.shard_map(
        on_device,
        mesh=mesh,
        in_specs=(
            P(None, "row", "col", None, None, None),
            P("row", "col", None, None, None),
            P("row", "col", None),
            P("row", "col", None),
            P("row", "col"),
            P("row", "col", None, None),
            P("row", "col", None, None),
        ),
        out_specs=P(None, "row", None, None, "col", None),
        check_vma=False,
    )
```
